256 devices in a mesh: grp: 8 (over y, core), pan: 32 (over z, x).
Axes of the slice: x: 4, y: 4, z: 8, core: 2. Of those that a mesh axis runs over, the one named last changes fastest.
Arguments:
- anc_rows: bfloat16 [16384, 16384], P('grp', 'pan'), as said below
- row_home: int32 [128], replicated, may hold values from 0 to 127, as said below
- block_lists: int32 [8, 64], replicated, may hold values from 0 to 127, as said below
- front_blocks: int32 [8], replicated, may hold values from 32 to 64, as said below
- panel: bfloat16 [8, 8192, 768], P('grp', 'pan'), may hold values from -0.29882812 to 0.29882812
- pivot_inverse: bfloat16 [8, 768, 768], P('grp'), as said below
Outputs:
- cross_cov: bfloat16 [8, 8192, 768], P('grp', 'pan')
- pivot_cov: float32 [8, 768, 768], P('grp', 'pan')
The draws below stay inside these ranges and needn't reach their ends.
Inputs may be any that keep to these rules, and one draw needn't show every extreme that they name: `row_home`: A permutation of 0 to 127; the 4 index blocks of each window [4 q, 4 q + 4) have their storage row blocks in one front group. `block_lists`: rising along each row; entries 2 * q to 2 * q + 1 lie in [4 * q, 4 * q + 4). `front_blocks`: some front has all 64 blocks. `anc_rows`: storage row block row_home[b] holds row block b of a symmetric matrix. `pivot_inverse`: lower triangular.
All inputs are finite; a program needn't handle non-finite values.
Results may differ from the reference program's by a relative error of at most 0.0095.
Values may be sent and summed in bfloat16 or wider, within the bound.
A program may use at most 128 MiB of HBM per device.

```python
import math
import jax
import jax.numpy as jnp
from jax import lax

BLK = 128
CB = 4
RB = 2
P_SIZE = 768
GROUPS = 8
NBA = 128
NA = 16384
PBG = 16
KB = 64
S = 8192
N_PAN = 32


def block_choice(key):
    base = jax.random.fold_in(key, 11)
    noise = jax.random.randint(base, (GROUPS, N_PAN, CB), 0, 1 << 20)
    scores = noise * CB + jnp.arange(CB, dtype=jnp.int32)
    ranked = jnp.argsort(scores, axis=-1)[..., :RB]
    chosen = jnp.sort(ranked, axis=-1).astype(jnp.int32)
    offsets = (jnp.arange(N_PAN, dtype=jnp.int32) * CB)[None, :, None]
    return (chosen + offsets).reshape(GROUPS, KB).astype(jnp.int32)


def slot_order(key):
    extra = jax.random.fold_in(key, 12)
    key_one, key_two = jax.random.split(extra)
    windows = NBA // CB
    window_perm = jax.random.permutation(key_one, windows).astype(jnp.int32)
    blocks = (window_perm[:, None] * CB + jnp.arange(CB, dtype=jnp.int32)[None, :]).reshape(NBA)
    ranks = jax.random.permutation(key_two, NBA).astype(jnp.int32)
    slot_group = jnp.arange(NBA, dtype=jnp.int32) // PBG
    scores = slot_group * NBA + ranks
    order = jnp.argsort(scores).astype(jnp.int32)
    return blocks[order].astype(jnp.int32)


def draw_block_lists(key, part):
    return block_choice(key)


def draw_row_home(key, part):
    return jnp.argsort(slot_order(key)).astype(jnp.int32)


def draw_front_blocks(key, part):
    base = jax.random.fold_in(key, 14)
    key_one, key_two = jax.random.split(base)
    counts = jax.random.randint(key_one, (GROUPS,), KB // 2, KB + 1)
    full_at = jax.random.randint(key_two, (), 0, GROUPS)
    return jnp.where(jnp.arange(GROUPS) == full_at, KB, counts).astype(jnp.int32)


def draw_anc_rows(key, part):
    slot_block = slot_order(key)
    base = jax.random.fold_in(key, 13)
    key_one, key_two = jax.random.split(base, 2)
    raw = jax.random.normal(key_one, (NA, NA), jnp.float32)
    symmetric = (raw + raw.T) * (0.7071 / math.sqrt(S))
    diag_vals = jax.random.uniform(key_two, (NA,), jnp.float32, 0.5, 1.5)
    index = jnp.arange(NA)
    symmetric = symmetric + jnp.where(index[:, None] == index[None, :], diag_vals[:, None], 0.0)
    stored = symmetric.reshape(NBA, BLK, NA)[slot_block].reshape(NA, NA)
    return stored.astype(jnp.bfloat16)


def draw_pivot_inverse(key, part):
    base = jax.random.fold_in(key, 15)
    key_one, key_two = jax.random.split(base)
    lower = jax.random.normal(key_one, (GROUPS, P_SIZE, P_SIZE), jnp.float32)
    lower = lower * (0.5 / math.sqrt(P_SIZE))
    index = jnp.arange(P_SIZE)
    lower = jnp.where(index[:, None] > index[None, :], lower, 0.0)
    diag_vals = jax.random.uniform(key_two, (GROUPS, P_SIZE), jnp.float32, 0.7, 1.4)
    result = lower + jnp.where(index[:, None] == index[None, :], diag_vals[:, :, None], 0.0)
    return result.astype(jnp.bfloat16)


def level_of(key, extent, shards, low, high):
    gain = 1.0
    for axis_at, shards_of in shards:
        heights = jax.random.uniform(jax.random.fold_in(jax.random.fold_in(key, 6), axis_at), (shards_of,), jnp.float32, low / len(shards), high / len(shards))
        gain = gain * jnp.repeat(jnp.exp(heights), extent[axis_at] // shards_of).reshape((-1,) + (1,) * (len(extent) - 1 - axis_at))
    return gain


def centred(own_key, shape, width, limit, pieces=(), held_as=jnp.bfloat16):
    entries = width * jax.random.normal(own_key, shape, jnp.float32)
    if pieces:
        entries = entries * level_of(own_key, shape, pieces, -0.22, 0.18)
    return jnp.clip(entries, -limit, limit).astype(held_as)


def setup_inputs(seed: int = 0) -> dict:
    keys = jax.random.split(jax.random.key(seed), 7)
    anc_rows = draw_anc_rows(jax.random.fold_in(keys[6], 71), 0)
    row_home = draw_row_home(jax.random.fold_in(keys[6], 71), 0)
    block_lists = draw_block_lists(jax.random.fold_in(keys[6], 71), 0)
    front_blocks = draw_front_blocks(jax.random.fold_in(keys[6], 71), 0)
    panel = centred(keys[4], (GROUPS, S, P_SIZE), 0.05, 0.29882812, ((0, 8), (1, 32)))
    pivot_inverse = draw_pivot_inverse(jax.random.fold_in(keys[6], 71), 0)
    return dict(anc_rows=anc_rows, row_home=row_home, block_lists=block_lists, front_blocks=front_blocks, panel=panel, pivot_inverse=pivot_inverse)


def reference(anc_rows, row_home, block_lists, front_blocks, panel, pivot_inverse):
    blocked = anc_rows.reshape(NBA, BLK, NA)
    contract = (((0,), (0,)), ((), ()))

    def front(group):
        members = block_lists[group]
        stripes = blocked[row_home[members]].reshape(S, NBA, BLK)
        sigma = stripes[:, members, :].reshape(S, S)
        alive = jnp.repeat(jnp.arange(KB, dtype=jnp.int32) < front_blocks[group], BLK)
        inverse_pivot = pivot_inverse[group]
        scaled = jnp.dot(panel[group], inverse_pivot, preferred_element_type=jnp.float32)
        scaled = jnp.where(alive[:, None], scaled, jnp.zeros_like(scaled)).astype(jnp.bfloat16)
        cross = -jnp.dot(sigma, scaled, preferred_element_type=jnp.float32)
        cross = jnp.where(alive[:, None], cross, jnp.zeros_like(cross)).astype(jnp.bfloat16)
        triangle = lax.dot_general(inverse_pivot, inverse_pivot, contract, preferred_element_type=jnp.float32)
        pivot = triangle - lax.dot_general(scaled, cross, contract, preferred_element_type=jnp.float32)
        return cross, pivot

    cross_cov, pivot_cov = lax.map(front, jnp.arange(GROUPS, dtype=jnp.int32))
    return cross_cov, pivot_cov
```

```python
import jax
import jax.numpy as jnp
from jax import lax
from jax.sharding import PartitionSpec as P

BLK = 128
P_SIZE = 768


def per_device(anc_rows, row_home, block_lists, front_blocks, panel, pivot_inverse):
    groups = lax.axis_size("grp")
    pan_count = lax.axis_size("pan")
    group_idx = lax.axis_index("grp")
    pan_idx = lax.axis_index("pan")
    block_count = row_home.shape[0]
    front_len = block_lists.shape[1]
    rb_local = front_len // pan_count
    cb_local = anc_rows.shape[1] // BLK
    stored_blocks = anc_rows.shape[0] // BLK
    windows = block_count // cb_local
    win_per_group = windows // groups
    per_src = win_per_group * rb_local
    contract = (((0,), (0,)), ((), ()))

    home_of_window = row_home[cb_local * jnp.arange(windows, dtype=jnp.int32)] // stored_blocks
    win = jnp.argsort(home_of_window * windows + jnp.arange(windows, dtype=jnp.int32))
    win = win.reshape(groups, win_per_group).astype(jnp.int32)
    pos = (rb_local * win[:, :, None] + jnp.arange(rb_local, dtype=jnp.int32)).reshape(
        groups, per_src
    )

    my_pos = lax.dynamic_index_in_dim(pos, group_idx, 0, keepdims=False)
    row_blocks = jnp.take(block_lists, my_pos, axis=1)
    slots = jnp.take(row_home, row_blocks) - stored_blocks * group_idx
    cols = lax.dynamic_slice_in_dim(block_lists, rb_local * pan_idx, rb_local, axis=1) - (
        cb_local * pan_idx
    )
    local = anc_rows.reshape(stored_blocks, BLK, cb_local, BLK)
    outgoing = local[slots[:, :, None], :, cols[:, None, :], :]
    received = lax.all_to_all(outgoing, "grp", split_axis=0, concat_axis=0, tiled=True)
    order = jnp.argsort(pos.reshape(groups * per_src)).astype(jnp.int32)
    sigma = jnp.take(received.reshape(groups * per_src, rb_local, BLK, BLK), order, axis=0)

    my_blocks = pan_idx * rb_local + jnp.arange(rb_local, dtype=jnp.int32)
    front_live = lax.dynamic_index_in_dim(front_blocks, group_idx, 0, keepdims=False)
    alive_rows = jnp.repeat(my_blocks < front_live, BLK)
    inverse_pivot = pivot_inverse[0]
    scaled = jnp.dot(panel[0], inverse_pivot, preferred_element_type=jnp.float32)
    scaled = jnp.where(alive_rows[:, None], scaled, jnp.zeros_like(scaled)).astype(jnp.bfloat16)
    full = lax.all_gather(scaled, "pan", axis=0, tiled=True)
    product = lax.dot_general(
        sigma,
        full.reshape(front_len, BLK, P_SIZE),
        (((0, 2), (0, 1)), ((), ())),
        preferred_element_type=jnp.float32,
    ).reshape(rb_local * BLK, P_SIZE)
    cross = jnp.where(alive_rows[:, None], -product, jnp.zeros_like(product)).astype(jnp.bfloat16)
    pivot_rows = P_SIZE // pan_count
    shared = lax.psum_scatter(
        (-lax.dot_general(scaled, cross, contract, preferred_element_type=jnp.float32)).astype(
            jnp.bfloat16
        ),
        "pan",
        scatter_dimension=0,
        tiled=True,
    ).astype(jnp.float32)
    own_columns = lax.dynamic_slice_in_dim(inverse_pivot, pan_idx * pivot_rows, pivot_rows, 1)
    triangle = lax.dot_general(
        own_columns, inverse_pivot, contract, preferred_element_type=jnp.float32
    )
    pivot = triangle + shared
    return (cross[None], pivot[None])


def solution(mesh):
    placed = (P("grp", "pan"), P(), P(), P(), P("grp", "pan", None), P("grp", None, None))
    return jax.shard_map(
        per_device,
        mesh=mesh,
        in_specs=placed,
        out_specs=(P("grp", "pan", None), P("grp", "pan", None)),
        check_vma=False,
    )
```

```python
import jax
import jax.numpy as jnp
from jax import lax
from jax.sharding import PartitionSpec as P
from jax.experimental import pallas as pl
from jax.experimental.pallas import tpu as pltpu

BLK = 128
P_SIZE = 768


def _scatter_sum_kernel(n, part_ref, out_ref, buf, send_sem, recv_sem, local_sem):
    me = lax.axis_index("pan")
    grp = lax.axis_index("grp")
    mesh_ids = pl.DeviceIdType.MESH

    barrier = pltpu.get_barrier_semaphore()

    def greet(k, carry):
        peer = lax.rem(me + k, n)
        pl.semaphore_signal(barrier, 1, device_id=(grp, peer), device_id_type=mesh_ids)
        return carry

    lax.fori_loop(1, n, greet, 0)
    pl.semaphore_wait(barrier, n - 1)

    own = pltpu.make_async_copy(part_ref.at[me], buf.at[0], local_sem)
    own.start()

    def send(k):
        peer = lax.rem(me + k, n)
        return pltpu.make_async_remote_copy(
            src_ref=part_ref.at[peer],
            dst_ref=buf.at[k],
            send_sem=send_sem.at[k],
            recv_sem=recv_sem.at[k],
            device_id=(grp, peer),
            device_id_type=mesh_ids,
        )

    def start(k, carry):
        send(k).start()
        return carry

    def finish(k, carry):
        send(k).wait()
        return carry

    lax.fori_loop(1, n, start, 0)
    own.wait()
    lax.fori_loop(1, n, finish, 0)

    out_ref[...] = buf[0].astype(jnp.float32)

    def accumulate(k, carry):
        out_ref[...] += buf[k].astype(jnp.float32)
        return carry

    lax.fori_loop(1, n, accumulate, 0)


def scatter_sum(part, n):
    _, rows, cols = part.shape
    return pl.pallas_call(
        lambda *refs: _scatter_sum_kernel(n, *refs),
        out_shape=jax.ShapeDtypeStruct((rows, cols), jnp.float32),
        in_specs=[pl.BlockSpec(memory_space=pl.ANY)],
        out_specs=pl.BlockSpec(memory_space=pltpu.VMEM),
        scratch_shapes=[
            pltpu.VMEM((n, rows, cols), part.dtype),
            pltpu.SemaphoreType.DMA((n,)),
            pltpu.SemaphoreType.DMA((n,)),
            pltpu.SemaphoreType.DMA,
        ],
        compiler_params=pltpu.CompilerParams(collective_id=0, has_side_effects=True),
    )(part)


def per_device(anc_rows, row_home, block_lists, front_blocks, panel, pivot_inverse):
    groups = lax.axis_size("grp")
    pan_count = lax.axis_size("pan")
    group_idx = lax.axis_index("grp")
    pan_idx = lax.axis_index("pan")
    block_count = row_home.shape[0]
    front_len = block_lists.shape[1]
    rb_local = front_len // pan_count
    cb_local = anc_rows.shape[1] // BLK
    stored_blocks = anc_rows.shape[0] // BLK
    windows = block_count // cb_local
    win_per_group = windows // groups
    per_src = win_per_group * rb_local
    contract = (((0,), (0,)), ((), ()))

    home_of_window = row_home[cb_local * jnp.arange(windows, dtype=jnp.int32)] // stored_blocks
    win = jnp.argsort(home_of_window * windows + jnp.arange(windows, dtype=jnp.int32))
    win = win.reshape(groups, win_per_group).astype(jnp.int32)
    pos = (rb_local * win[:, :, None] + jnp.arange(rb_local, dtype=jnp.int32)).reshape(
        groups, per_src
    )

    my_pos = lax.dynamic_index_in_dim(pos, group_idx, 0, keepdims=False)
    row_blocks = jnp.take(block_lists, my_pos, axis=1)
    slots = jnp.take(row_home, row_blocks) - stored_blocks * group_idx
    cols = lax.dynamic_slice_in_dim(block_lists, rb_local * pan_idx, rb_local, axis=1) - (
        cb_local * pan_idx
    )
    local = anc_rows.reshape(stored_blocks, BLK, cb_local, BLK)
    outgoing = local[slots[:, :, None], :, cols[:, None, :], :]
    received = lax.all_to_all(outgoing, "grp", split_axis=0, concat_axis=0, tiled=True)
    order = jnp.argsort(pos.reshape(groups * per_src)).astype(jnp.int32)
    sigma = jnp.take(received.reshape(groups * per_src, rb_local, BLK, BLK), order, axis=0)

    my_blocks = pan_idx * rb_local + jnp.arange(rb_local, dtype=jnp.int32)
    front_live = lax.dynamic_index_in_dim(front_blocks, group_idx, 0, keepdims=False)
    alive_rows = jnp.repeat(my_blocks < front_live, BLK)
    inverse_pivot = pivot_inverse[0]
    scaled = jnp.dot(panel[0], inverse_pivot, preferred_element_type=jnp.float32)
    scaled = jnp.where(alive_rows[:, None], scaled, jnp.zeros_like(scaled)).astype(jnp.bfloat16)
    full = lax.all_gather(scaled, "pan", axis=0, tiled=True)
    product = lax.dot_general(
        sigma,
        full.reshape(front_len, BLK, P_SIZE),
        (((0, 2), (0, 1)), ((), ())),
        preferred_element_type=jnp.float32,
    ).reshape(rb_local * BLK, P_SIZE)
    cross = jnp.where(alive_rows[:, None], -product, jnp.zeros_like(product)).astype(jnp.bfloat16)
    pivot_rows = P_SIZE // pan_count
    part = (-lax.dot_general(scaled, cross, contract, preferred_element_type=jnp.float32)).astype(
        jnp.bfloat16
    )
    shared = scatter_sum(part.reshape(pan_count, pivot_rows, P_SIZE), pan_count)
    own_columns = lax.dynamic_slice_in_dim(inverse_pivot, pan_idx * pivot_rows, pivot_rows, 1)
    triangle = lax.dot_general(
        own_columns, inverse_pivot, contract, preferred_element_type=jnp.float32
    )
    pivot = triangle + shared
    return (cross[None], pivot[None])


def solution(mesh):
    placed = (P("grp", "pan"), P(), P(), P(), P("grp", "pan", None), P("grp", None, None))
    return jax.shard_map(
        per_device,
        mesh=mesh,
        in_specs=placed,
        out_specs=(P("grp", "pan", None), P("grp", "pan", None)),
        check_vma=False,
    )
```

```python
import jax
import jax.numpy as jnp
from jax import lax
from jax.sharding import PartitionSpec as P
from jax.experimental import pallas as pl
from jax.experimental.pallas import tpu as pltpu

BLK = 128
P_SIZE = 768


def _scatter_sum_kernel(n, part_ref, out_ref, buf, send_sem, recv_sem, local_sem):
    me = lax.axis_index("pan")
    grp = lax.axis_index("grp")
    mesh_ids = pl.DeviceIdType.MESH

    barrier = pltpu.get_barrier_semaphore()

    def greet(k, carry):
        peer = lax.rem(me + k, n)
        pl.semaphore_signal(barrier, 1, device_id=(grp, peer), device_id_type=mesh_ids)
        return carry

    lax.fori_loop(1, n, greet, 0)
    pl.semaphore_wait(barrier, n - 1)

    own = pltpu.make_async_copy(part_ref.at[me], buf.at[0], local_sem)
    own.start()

    def send(k):
        peer = lax.rem(me + k, n)
        return pltpu.make_async_remote_copy(
            src_ref=part_ref.at[peer],
            dst_ref=buf.at[k],
            send_sem=send_sem.at[k],
            recv_sem=recv_sem.at[k],
            device_id=(grp, peer),
            device_id_type=mesh_ids,
        )

    def start(k, carry):
        send(k).start()
        return carry

    def finish(k, carry):
        send(k).wait()
        return carry

    lax.fori_loop(1, n, start, 0)
    own.wait()
    lax.fori_loop(1, n, finish, 0)

    out_ref[...] = buf[0].astype(jnp.float32)

    def accumulate(k, carry):
        out_ref[...] += buf[k].astype(jnp.float32)
        return carry

    lax.fori_loop(1, n, accumulate, 0)


def scatter_sum(part, n, kernel_id):
    _, rows, cols = part.shape
    return pl.pallas_call(
        lambda *refs: _scatter_sum_kernel(n, *refs),
        out_shape=jax.ShapeDtypeStruct((rows, cols), jnp.float32),
        in_specs=[pl.BlockSpec(memory_space=pl.ANY)],
        out_specs=pl.BlockSpec(memory_space=pltpu.VMEM),
        scratch_shapes=[
            pltpu.VMEM((n, rows, cols), part.dtype),
            pltpu.SemaphoreType.DMA((n,)),
            pltpu.SemaphoreType.DMA((n,)),
            pltpu.SemaphoreType.DMA,
        ],
        compiler_params=pltpu.CompilerParams(collective_id=kernel_id, has_side_effects=True),
        cost_estimate=pl.CostEstimate(
            flops=n * rows * cols,
            bytes_accessed=2 * n * rows * cols * part.dtype.itemsize,
            transcendentals=0,
        ),
    )(part)


def per_device(anc_rows, row_home, block_lists, front_blocks, panel, pivot_inverse):
    groups = lax.axis_size("grp")
    pan_count = lax.axis_size("pan")
    group_idx = lax.axis_index("grp")
    pan_idx = lax.axis_index("pan")
    block_count = row_home.shape[0]
    front_len = block_lists.shape[1]
    rb_local = front_len // pan_count
    cb_local = anc_rows.shape[1] // BLK
    stored_blocks = anc_rows.shape[0] // BLK
    windows = block_count // cb_local
    win_per_group = windows // groups
    per_src = win_per_group * rb_local
    contract = (((0,), (0,)), ((), ()))

    home_of_window = row_home[cb_local * jnp.arange(windows, dtype=jnp.int32)] // stored_blocks
    win = jnp.argsort(home_of_window * windows + jnp.arange(windows, dtype=jnp.int32))
    win = win.reshape(groups, win_per_group).astype(jnp.int32)
    pos = (rb_local * win[:, :, None] + jnp.arange(rb_local, dtype=jnp.int32)).reshape(
        groups, per_src
    )

    my_pos = lax.dynamic_index_in_dim(pos, group_idx, 0, keepdims=False)
    row_blocks = jnp.take(block_lists, my_pos, axis=1)
    slots = jnp.take(row_home, row_blocks) - stored_blocks * group_idx
    cols = lax.dynamic_slice_in_dim(block_lists, rb_local * pan_idx, rb_local, axis=1) - (
        cb_local * pan_idx
    )
    local = anc_rows.reshape(stored_blocks, BLK, cb_local, BLK)
    outgoing = local[slots[:, :, None], :, cols[:, None, :], :]
    received = lax.all_to_all(outgoing, "grp", split_axis=0, concat_axis=0, tiled=True)
    order = jnp.argsort(pos.reshape(groups * per_src)).astype(jnp.int32)
    sigma = jnp.take(received.reshape(groups * per_src, rb_local, BLK, BLK), order, axis=0)

    my_blocks = pan_idx * rb_local + jnp.arange(rb_local, dtype=jnp.int32)
    front_live = lax.dynamic_index_in_dim(front_blocks, group_idx, 0, keepdims=False)
    alive_rows = jnp.repeat(my_blocks < front_live, BLK)
    inverse_pivot = pivot_inverse[0]
    scaled = jnp.dot(panel[0], inverse_pivot, preferred_element_type=jnp.float32)
    scaled = jnp.where(alive_rows[:, None], scaled, jnp.zeros_like(scaled)).astype(jnp.bfloat16)
    pivot_rows = P_SIZE // pan_count
    cross_pieces = []
    shared_pieces = []
    first = 0
    for piece, width in enumerate((P_SIZE // 3, 2 * P_SIZE // 3)):
        full = lax.all_gather(scaled[:, first : first + width], "pan", axis=0, tiled=True)
        product = lax.dot_general(
            sigma,
            full.reshape(front_len, BLK, width),
            (((0, 2), (0, 1)), ((), ())),
            preferred_element_type=jnp.float32,
        ).reshape(rb_local * BLK, width)
        cross_piece = jnp.where(
            alive_rows[:, None], -product, jnp.zeros_like(product)
        ).astype(jnp.bfloat16)
        part = (
            -lax.dot_general(scaled, cross_piece, contract, preferred_element_type=jnp.float32)
        ).astype(jnp.bfloat16)
        slabs = part.reshape(pan_count, pivot_rows * width // BLK, BLK)
        summed = scatter_sum(slabs, pan_count, piece)
        cross_pieces.append(cross_piece)
        shared_pieces.append(summed.reshape(pivot_rows, width))
        first += width
    cross = jnp.concatenate(cross_pieces, axis=1)
    shared = jnp.concatenate(shared_pieces, axis=1)
    own_columns = lax.dynamic_slice_in_dim(inverse_pivot, pan_idx * pivot_rows, pivot_rows, 1)
    triangle = lax.dot_general(
        own_columns, inverse_pivot, contract, preferred_element_type=jnp.float32
    )
    pivot = triangle + shared
    return (cross[None], pivot[None])


def solution(mesh):
    placed = (P("grp", "pan"), P(), P(), P(), P("grp", "pan", None), P("grp", None, None))
    return jax.shard_map(
        per_device,
        mesh=mesh,
        in_specs=placed,
        out_specs=(P("grp", "pan", None), P("grp", "pan", None)),
        check_vma=False,
    )
```

```python
import jax
import jax.numpy as jnp
from jax import lax
from jax.sharding import PartitionSpec as P
from jax.experimental import pallas as pl
from jax.experimental.pallas import tpu as pltpu

BLK = 128
P_SIZE = 768


def _scatter_sum_kernel(n, part_ref, base_ref, out_ref, buf, send_sem, recv_sem, local_sem):
    me = lax.axis_index("pan")
    grp = lax.axis_index("grp")
    mesh_ids = pl.DeviceIdType.MESH

    barrier = pltpu.get_barrier_semaphore()

    def greet(k, carry):
        peer = lax.rem(me + k, n)
        pl.semaphore_signal(barrier, 1, device_id=(grp, peer), device_id_type=mesh_ids)
        return carry

    lax.fori_loop(1, n, greet, 0)
    pl.semaphore_wait(barrier, n - 1)

    own = pltpu.make_async_copy(part_ref.at[me], buf.at[0], local_sem)
    own.start()

    def send(k):
        peer = lax.rem(me + k, n)
        return pltpu.make_async_remote_copy(
            src_ref=part_ref.at[peer],
            dst_ref=buf.at[k],
            send_sem=send_sem.at[k],
            recv_sem=recv_sem.at[k],
            device_id=(grp, peer),
            device_id_type=mesh_ids,
        )

    def start(k, carry):
        send(k).start()
        return carry

    def finish(k, carry):
        send(k).wait()
        return carry

    lax.fori_loop(1, n, start, 0)
    own.wait()
    lax.fori_loop(1, n, finish, 0)

    out_ref[...] = base_ref[...] + buf[0].astype(jnp.float32)

    def accumulate(k, carry):
        out_ref[...] += buf[k].astype(jnp.float32)
        return carry

    lax.fori_loop(1, n, accumulate, 0)


def scatter_sum(part, base, n):
    _, rows, cols = part.shape
    return pl.pallas_call(
        lambda *refs: _scatter_sum_kernel(n, *refs),
        out_shape=jax.ShapeDtypeStruct((rows, cols), jnp.float32),
        in_specs=[pl.BlockSpec(memory_space=pl.ANY), pl.BlockSpec(memory_space=pltpu.VMEM)],
        out_specs=pl.BlockSpec(memory_space=pltpu.VMEM),
        scratch_shapes=[
            pltpu.VMEM((n, rows, cols), part.dtype),
            pltpu.SemaphoreType.DMA((n,)),
            pltpu.SemaphoreType.DMA((n,)),
            pltpu.SemaphoreType.DMA,
        ],
        compiler_params=pltpu.CompilerParams(collective_id=0, has_side_effects=True),
    )(part, base)


def per_device(anc_rows, row_home, block_lists, front_blocks, panel, pivot_inverse):
    groups = lax.axis_size("grp")
    pan_count = lax.axis_size("pan")
    group_idx = lax.axis_index("grp")
    pan_idx = lax.axis_index("pan")
    block_count = row_home.shape[0]
    front_len = block_lists.shape[1]
    rb_local = front_len // pan_count
    cb_local = anc_rows.shape[1] // BLK
    stored_blocks = anc_rows.shape[0] // BLK
    windows = block_count // cb_local
    win_per_group = windows // groups
    per_src = win_per_group * rb_local
    contract = (((0,), (0,)), ((), ()))

    home_of_window = row_home[cb_local * jnp.arange(windows, dtype=jnp.int32)] // stored_blocks
    win = jnp.argsort(home_of_window * windows + jnp.arange(windows, dtype=jnp.int32))
    win = win.reshape(groups, win_per_group).astype(jnp.int32)
    pos = (rb_local * win[:, :, None] + jnp.arange(rb_local, dtype=jnp.int32)).reshape(
        groups, per_src
    )

    my_pos = lax.dynamic_index_in_dim(pos, group_idx, 0, keepdims=False)
    row_blocks = jnp.take(block_lists, my_pos, axis=1)
    slots = jnp.take(row_home, row_blocks) - stored_blocks * group_idx
    cols = lax.dynamic_slice_in_dim(block_lists, rb_local * pan_idx, rb_local, axis=1) - (
        cb_local * pan_idx
    )
    local = anc_rows.reshape(stored_blocks, BLK, cb_local, BLK)
    outgoing = local[slots[:, :, None], :, cols[:, None, :], :]
    received = lax.all_to_all(outgoing, "grp", split_axis=0, concat_axis=0, tiled=True)
    order = jnp.argsort(pos.reshape(groups * per_src)).astype(jnp.int32)
    sigma = jnp.take(received.reshape(groups * per_src, rb_local, BLK, BLK), order, axis=0)
    sigma_t = jnp.transpose(sigma, (1, 3, 0, 2)).reshape(rb_local * BLK, front_len * BLK)

    my_blocks = pan_idx * rb_local + jnp.arange(rb_local, dtype=jnp.int32)
    front_live = lax.dynamic_index_in_dim(front_blocks, group_idx, 0, keepdims=False)
    alive_rows = jnp.repeat(my_blocks < front_live, BLK)
    inverse_pivot = pivot_inverse[0]
    scaled = jnp.dot(panel[0], inverse_pivot, preferred_element_type=jnp.float32)
    scaled = jnp.where(alive_rows[:, None], scaled, jnp.zeros_like(scaled)).astype(jnp.bfloat16)
    full = lax.all_gather(scaled, "pan", axis=0, tiled=True)
    product = jnp.dot(sigma_t, full, preferred_element_type=jnp.float32)
    cross = jnp.where(alive_rows[:, None], -product, jnp.zeros_like(product)).astype(jnp.bfloat16)
    pivot_rows = P_SIZE // pan_count
    part = (-lax.dot_general(scaled, cross, contract, preferred_element_type=jnp.float32)).astype(
        jnp.bfloat16
    )
    own_columns = lax.dynamic_slice_in_dim(inverse_pivot, pan_idx * pivot_rows, pivot_rows, 1)
    triangle = lax.dot_general(
        own_columns, inverse_pivot, contract, preferred_element_type=jnp.float32
    )
    pivot = scatter_sum(part.reshape(pan_count, pivot_rows, P_SIZE), triangle, pan_count)
    return (cross[None], pivot[None])


def solution(mesh):
    placed = (P("grp", "pan"), P(), P(), P(), P("grp", "pan", None), P("grp", None, None))
    return jax.shard_map(
        per_device,
        mesh=mesh,
        in_specs=placed,
        out_specs=(P("grp", "pan", None), P("grp", "pan", None)),
        check_vma=False,
    )
```

```python
import jax
import jax.numpy as jnp
from jax import lax
from jax.sharding import PartitionSpec as P
from jax.experimental import pallas as pl
from jax.experimental.pallas import tpu as pltpu

BLK = 128
P_SIZE = 768


def _scatter_sum_kernel(n, part_ref, out_ref, buf, send_sem, recv_sem, local_sem):
    me = lax.axis_index("pan")
    grp = lax.axis_index("grp")
    mesh_ids = pl.DeviceIdType.MESH

    barrier = pltpu.get_barrier_semaphore()

    def greet(k, carry):
        peer = lax.rem(me + k, n)
        pl.semaphore_signal(barrier, 1, device_id=(grp, peer), device_id_type=mesh_ids)
        return carry

    lax.fori_loop(1, n, greet, 0)
    pl.semaphore_wait(barrier, n - 1)

    own = pltpu.make_async_copy(part_ref.at[me], buf.at[0], local_sem)
    own.start()

    def send(k):
        peer = lax.rem(me + k, n)
        return pltpu.make_async_remote_copy(
            src_ref=part_ref.at[peer],
            dst_ref=buf.at[k],
            send_sem=send_sem.at[k],
            recv_sem=recv_sem.at[k],
            device_id=(grp, peer),
            device_id_type=mesh_ids,
        )

    def start(k, carry):
        send(k).start()
        return carry

    def finish(k, carry):
        send(k).wait()
        return carry

    lax.fori_loop(1, n, start, 0)
    own.wait()
    lax.fori_loop(1, n, finish, 0)

    out_ref[...] = buf[0].astype(jnp.float32)

    def accumulate(k, carry):
        out_ref[...] += buf[k].astype(jnp.float32)
        return carry

    lax.fori_loop(1, n, accumulate, 0)


def scatter_sum(part, n):
    _, rows, cols = part.shape
    return pl.pallas_call(
        lambda *refs: _scatter_sum_kernel(n, *refs),
        out_shape=jax.ShapeDtypeStruct((rows, cols), jnp.float32),
        in_specs=[pl.BlockSpec(memory_space=pl.ANY)],
        out_specs=pl.BlockSpec(memory_space=pltpu.VMEM),
        scratch_shapes=[
            pltpu.VMEM((n, rows, cols), part.dtype),
            pltpu.SemaphoreType.DMA((n,)),
            pltpu.SemaphoreType.DMA((n,)),
            pltpu.SemaphoreType.DMA,
        ],
        compiler_params=pltpu.CompilerParams(collective_id=0, has_side_effects=True),
    )(part)


def per_device(anc_rows, row_home, block_lists, front_blocks, panel, pivot_inverse):
    groups = lax.axis_size("grp")
    pan_count = lax.axis_size("pan")
    group_idx = lax.axis_index("grp")
    pan_idx = lax.axis_index("pan")
    block_count = row_home.shape[0]
    front_len = block_lists.shape[1]
    rb_local = front_len // pan_count
    cb_local = anc_rows.shape[1] // BLK
    stored_blocks = anc_rows.shape[0] // BLK
    windows = block_count // cb_local
    win_per_group = windows // groups
    per_src = win_per_group * rb_local
    contract = (((0,), (0,)), ((), ()))

    home_of_window = row_home[cb_local * jnp.arange(windows, dtype=jnp.int32)] // stored_blocks
    win = jnp.argsort(home_of_window * windows + jnp.arange(windows, dtype=jnp.int32))
    win = win.reshape(groups, win_per_group).astype(jnp.int32)
    pos = (rb_local * win[:, :, None] + jnp.arange(rb_local, dtype=jnp.int32)).reshape(
        groups, per_src
    )

    my_pos = lax.dynamic_index_in_dim(pos, group_idx, 0, keepdims=False)
    row_blocks = jnp.take(block_lists, my_pos, axis=1)
    slots = jnp.take(row_home, row_blocks) - stored_blocks * group_idx
    cols = lax.dynamic_slice_in_dim(block_lists, rb_local * pan_idx, rb_local, axis=1) - (
        cb_local * pan_idx
    )
    local = anc_rows.reshape(stored_blocks, BLK, cb_local, BLK)
    outgoing = local[slots[:, :, None], :, cols[:, None, :], :]
    received = lax.all_to_all(outgoing, "grp", split_axis=0, concat_axis=0, tiled=True)
    order = jnp.argsort(pos.reshape(groups * per_src)).astype(jnp.int32)
    sigma = jnp.take(received.reshape(groups * per_src, rb_local, BLK, BLK), order, axis=0)

    my_blocks = pan_idx * rb_local + jnp.arange(rb_local, dtype=jnp.int32)
    front_live = lax.dynamic_index_in_dim(front_blocks, group_idx, 0, keepdims=False)
    alive_rows = jnp.repeat(my_blocks < front_live, BLK)
    inverse_pivot = pivot_inverse[0]
    scaled = jnp.dot(panel[0], inverse_pivot, preferred_element_type=jnp.float32)
    scaled = jnp.where(alive_rows[:, None], scaled, jnp.zeros_like(scaled)).astype(jnp.bfloat16)
    full = lax.all_gather(scaled, "pan", axis=0, tiled=True)
    product = lax.dot_general(
        sigma,
        full.reshape(front_len, BLK, P_SIZE),
        (((0, 2), (0, 1)), ((), ())),
        preferred_element_type=jnp.float32,
    ).reshape(rb_local * BLK, P_SIZE)
    cross = jnp.where(alive_rows[:, None], -product, jnp.zeros_like(product)).astype(jnp.bfloat16)
    pivot_rows = P_SIZE // pan_count
    part = (-lax.dot_general(scaled, cross, contract, preferred_element_type=jnp.float32)).astype(
        jnp.bfloat16
    )
    slab_rows = pivot_rows * P_SIZE // BLK
    shared = scatter_sum(part.reshape(pan_count, slab_rows, BLK), pan_count).reshape(
        pivot_rows, P_SIZE
    )
    own_columns = lax.dynamic_slice_in_dim(inverse_pivot, pan_idx * pivot_rows, pivot_rows, 1)
    triangle = lax.dot_general(
        own_columns, inverse_pivot, contract, preferred_element_type=jnp.float32
    )
    pivot = triangle + shared
    return (cross[None], pivot[None])


def solution(mesh):
    placed = (P("grp", "pan"), P(), P(), P(), P("grp", "pan", None), P("grp", None, None))
    return jax.shard_map(
        per_device,
        mesh=mesh,
        in_specs=placed,
        out_specs=(P("grp", "pan", None), P("grp", "pan", None)),
        check_vma=False,
    )
```

```python
import jax
import jax.numpy as jnp
from jax import lax
from jax.sharding import PartitionSpec as P
from jax.experimental import pallas as pl
from jax.experimental.pallas import tpu as pltpu

BLK = 128
P_SIZE = 768


def _scatter_sum_kernel(n, part_ref, out_ref, buf, send_sem, recv_sem, local_sem):
    me = lax.axis_index("pan")
    grp = lax.axis_index("grp")
    mesh_ids = pl.DeviceIdType.MESH

    own = pltpu.make_async_copy(part_ref.at[me], buf.at[0], local_sem)
    own.start()

    def send(k):
        peer = lax.rem(me + k, n)
        return pltpu.make_async_remote_copy(
            src_ref=part_ref.at[peer],
            dst_ref=buf.at[k],
            send_sem=send_sem.at[k],
            recv_sem=recv_sem.at[k],
            device_id=(grp, peer),
            device_id_type=mesh_ids,
        )

    def start(k, carry):
        send(k).start()
        return carry

    def finish(k, carry):
        send(k).wait()
        return carry

    lax.fori_loop(1, n, start, 0)
    own.wait()
    lax.fori_loop(1, n, finish, 0)

    out_ref[...] = buf[0].astype(jnp.float32)

    def accumulate(k, carry):
        out_ref[...] += buf[k].astype(jnp.float32)
        return carry

    lax.fori_loop(1, n, accumulate, 0)


def scatter_sum(part, n):
    _, rows, cols = part.shape
    return pl.pallas_call(
        lambda *refs: _scatter_sum_kernel(n, *refs),
        out_shape=jax.ShapeDtypeStruct((rows, cols), jnp.float32),
        in_specs=[pl.BlockSpec(memory_space=pl.ANY)],
        out_specs=pl.BlockSpec(memory_space=pltpu.VMEM),
        scratch_shapes=[
            pltpu.VMEM((n, rows, cols), part.dtype),
            pltpu.SemaphoreType.DMA((n,)),
            pltpu.SemaphoreType.DMA((n,)),
            pltpu.SemaphoreType.DMA,
        ],
        compiler_params=pltpu.CompilerParams(has_side_effects=True),
    )(part)


def per_device(anc_rows, row_home, block_lists, front_blocks, panel, pivot_inverse):
    groups = lax.axis_size("grp")
    pan_count = lax.axis_size("pan")
    group_idx = lax.axis_index("grp")
    pan_idx = lax.axis_index("pan")
    block_count = row_home.shape[0]
    front_len = block_lists.shape[1]
    rb_local = front_len // pan_count
    cb_local = anc_rows.shape[1] // BLK
    stored_blocks = anc_rows.shape[0] // BLK
    windows = block_count // cb_local
    win_per_group = windows // groups
    per_src = win_per_group * rb_local
    contract = (((0,), (0,)), ((), ()))

    home_of_window = row_home[cb_local * jnp.arange(windows, dtype=jnp.int32)] // stored_blocks
    win = jnp.argsort(home_of_window * windows + jnp.arange(windows, dtype=jnp.int32))
    win = win.reshape(groups, win_per_group).astype(jnp.int32)
    pos = (rb_local * win[:, :, None] + jnp.arange(rb_local, dtype=jnp.int32)).reshape(
        groups, per_src
    )

    my_pos = lax.dynamic_index_in_dim(pos, group_idx, 0, keepdims=False)
    row_blocks = jnp.take(block_lists, my_pos, axis=1)
    slots = jnp.take(row_home, row_blocks) - stored_blocks * group_idx
    cols = lax.dynamic_slice_in_dim(block_lists, rb_local * pan_idx, rb_local, axis=1) - (
        cb_local * pan_idx
    )
    local = anc_rows.reshape(stored_blocks, BLK, cb_local, BLK)
    outgoing = local[slots[:, :, None], :, cols[:, None, :], :]
    received = lax.all_to_all(outgoing, "grp", split_axis=0, concat_axis=0, tiled=True)
    order = jnp.argsort(pos.reshape(groups * per_src)).astype(jnp.int32)
    sigma = jnp.take(received.reshape(groups * per_src, rb_local, BLK, BLK), order, axis=0)

    my_blocks = pan_idx * rb_local + jnp.arange(rb_local, dtype=jnp.int32)
    front_live = lax.dynamic_index_in_dim(front_blocks, group_idx, 0, keepdims=False)
    alive_rows = jnp.repeat(my_blocks < front_live, BLK)
    inverse_pivot = pivot_inverse[0]
    scaled = jnp.dot(panel[0], inverse_pivot, preferred_element_type=jnp.float32)
    scaled = jnp.where(alive_rows[:, None], scaled, jnp.zeros_like(scaled)).astype(jnp.bfloat16)
    full = lax.all_gather(scaled, "pan", axis=0, tiled=True)
    product = lax.dot_general(
        sigma,
        full.reshape(front_len, BLK, P_SIZE),
        (((0, 2), (0, 1)), ((), ())),
        preferred_element_type=jnp.float32,
    ).reshape(rb_local * BLK, P_SIZE)
    cross = jnp.where(alive_rows[:, None], -product, jnp.zeros_like(product)).astype(jnp.bfloat16)
    pivot_rows = P_SIZE // pan_count
    part = (-lax.dot_general(scaled, cross, contract, preferred_element_type=jnp.float32)).astype(
        jnp.bfloat16
    )
    shared = scatter_sum(part.reshape(pan_count, pivot_rows, P_SIZE), pan_count)
    own_columns = lax.dynamic_slice_in_dim(inverse_pivot, pan_idx * pivot_rows, pivot_rows, 1)
    triangle = lax.dot_general(
        own_columns, inverse_pivot, contract, preferred_element_type=jnp.float32
    )
    pivot = triangle + shared
    return (cross[None], pivot[None])


def solution(mesh):
    placed = (P("grp", "pan"), P(), P(), P(), P("grp", "pan", None), P("grp", None, None))
    return jax.shard_map(
        per_device,
        mesh=mesh,
        in_specs=placed,
        out_specs=(P("grp", "pan", None), P("grp", "pan", None)),
        check_vma=False,
    )
```

```python
import functools

import jax
import jax.numpy as jnp
from jax import lax
from jax.sharding import PartitionSpec as P
from jax.experimental import pallas as pl
from jax.experimental.pallas import tpu as pltpu

BLK = 128
P_SIZE = 768


PAN_INNER = 4


def _scatter_sum_kernel(
    inner, outer, part_ref, out_ref, first, mid, second, sems, local_sem
):
    me = lax.axis_index("pan")
    grp = lax.axis_index("grp")
    row, col = me // inner, me % inner
    mesh_ids = pl.DeviceIdType.MESH
    send1, recv1, send2, recv2 = sems

    barrier = pltpu.get_barrier_semaphore()

    def greet_row(k, carry):
        peer = row * inner + lax.rem(col + k, inner)
        pl.semaphore_signal(barrier, 1, device_id=(grp, peer), device_id_type=mesh_ids)
        return carry

    def greet_col(k, carry):
        peer = lax.rem(row + k, outer) * inner + col
        pl.semaphore_signal(barrier, 1, device_id=(grp, peer), device_id_type=mesh_ids)
        return carry

    lax.fori_loop(1, inner, greet_row, 0)
    lax.fori_loop(1, outer, greet_col, 0)
    pl.semaphore_wait(barrier, inner + outer - 2)

    own = pltpu.make_async_copy(part_ref.at[:, col], first.at[0], local_sem)
    own.start()

    def stage_one(k):
        dest = lax.rem(col + k, inner)
        return pltpu.make_async_remote_copy(
            src_ref=part_ref.at[:, dest],
            dst_ref=first.at[k],
            send_sem=send1.at[k],
            recv_sem=recv1.at[k],
            device_id=(grp, row * inner + dest),
            device_id_type=mesh_ids,
        )

    def start_one(k, carry):
        stage_one(k).start()
        return carry

    def finish_one(k, carry):
        stage_one(k).wait()
        return carry

    lax.fori_loop(1, inner, start_one, 0)
    own.wait()
    lax.fori_loop(1, inner, finish_one, 0)

    mid[...] = first[0].astype(jnp.float32)

    def add_first(k, carry):
        mid[...] += first[k].astype(jnp.float32)
        return carry

    lax.fori_loop(1, inner, add_first, 0)

    def stage_two(k):
        dest = lax.rem(row + k, outer)
        return pltpu.make_async_remote_copy(
            src_ref=mid.at[dest],
            dst_ref=second.at[k],
            send_sem=send2.at[k],
            recv_sem=recv2.at[k],
            device_id=(grp, dest * inner + col),
            device_id_type=mesh_ids,
        )

    def start_two(k, carry):
        stage_two(k).start()
        return carry

    def finish_two(k, carry):
        stage_two(k).wait()
        return carry

    lax.fori_loop(1, outer, start_two, 0)
    lax.fori_loop(1, outer, finish_two, 0)

    out_ref[...] = mid[row]

    def add_second(k, carry):
        out_ref[...] += second[k]
        return carry

    lax.fori_loop(1, outer, add_second, 0)


def scatter_sum(part, n):
    _, rows, cols = part.shape
    inner = PAN_INNER
    outer = n // inner
    return pl.pallas_call(
        functools.partial(_scatter_sum_kernel, inner, outer),
        out_shape=jax.ShapeDtypeStruct((rows, cols), jnp.float32),
        in_specs=[pl.BlockSpec(memory_space=pl.ANY)],
        out_specs=pl.BlockSpec(memory_space=pltpu.VMEM),
        scratch_shapes=[
            pltpu.VMEM((inner, outer, rows, cols), part.dtype),
            pltpu.VMEM((outer, rows, cols), jnp.float32),
            pltpu.VMEM((outer, rows, cols), jnp.float32),
            (
                pltpu.SemaphoreType.DMA((inner,)),
                pltpu.SemaphoreType.DMA((inner,)),
                pltpu.SemaphoreType.DMA((outer,)),
                pltpu.SemaphoreType.DMA((outer,)),
            ),
            pltpu.SemaphoreType.DMA,
        ],
        compiler_params=pltpu.CompilerParams(collective_id=0, has_side_effects=True),
    )(part.reshape(outer, inner, rows, cols))


def per_device(anc_rows, row_home, block_lists, front_blocks, panel, pivot_inverse):
    groups = lax.axis_size("grp")
    pan_count = lax.axis_size("pan")
    group_idx = lax.axis_index("grp")
    pan_idx = lax.axis_index("pan")
    block_count = row_home.shape[0]
    front_len = block_lists.shape[1]
    rb_local = front_len // pan_count
    cb_local = anc_rows.shape[1] // BLK
    stored_blocks = anc_rows.shape[0] // BLK
    windows = block_count // cb_local
    win_per_group = windows // groups
    per_src = win_per_group * rb_local
    contract = (((0,), (0,)), ((), ()))

    home_of_window = row_home[cb_local * jnp.arange(windows, dtype=jnp.int32)] // stored_blocks
    win = jnp.argsort(home_of_window * windows + jnp.arange(windows, dtype=jnp.int32))
    win = win.reshape(groups, win_per_group).astype(jnp.int32)
    pos = (rb_local * win[:, :, None] + jnp.arange(rb_local, dtype=jnp.int32)).reshape(
        groups, per_src
    )

    my_pos = lax.dynamic_index_in_dim(pos, group_idx, 0, keepdims=False)
    row_blocks = jnp.take(block_lists, my_pos, axis=1)
    slots = jnp.take(row_home, row_blocks) - stored_blocks * group_idx
    cols = lax.dynamic_slice_in_dim(block_lists, rb_local * pan_idx, rb_local, axis=1) - (
        cb_local * pan_idx
    )
    local = anc_rows.reshape(stored_blocks, BLK, cb_local, BLK)
    outgoing = local[slots[:, :, None], :, cols[:, None, :], :]
    received = lax.all_to_all(outgoing, "grp", split_axis=0, concat_axis=0, tiled=True)
    order = jnp.argsort(pos.reshape(groups * per_src)).astype(jnp.int32)
    sigma = jnp.take(received.reshape(groups * per_src, rb_local, BLK, BLK), order, axis=0)

    my_blocks = pan_idx * rb_local + jnp.arange(rb_local, dtype=jnp.int32)
    front_live = lax.dynamic_index_in_dim(front_blocks, group_idx, 0, keepdims=False)
    alive_rows = jnp.repeat(my_blocks < front_live, BLK)
    inverse_pivot = pivot_inverse[0]
    scaled = jnp.dot(panel[0], inverse_pivot, preferred_element_type=jnp.float32)
    scaled = jnp.where(alive_rows[:, None], scaled, jnp.zeros_like(scaled)).astype(jnp.bfloat16)
    full = lax.all_gather(scaled, "pan", axis=0, tiled=True)
    product = lax.dot_general(
        sigma,
        full.reshape(front_len, BLK, P_SIZE),
        (((0, 2), (0, 1)), ((), ())),
        preferred_element_type=jnp.float32,
    ).reshape(rb_local * BLK, P_SIZE)
    cross = jnp.where(alive_rows[:, None], -product, jnp.zeros_like(product)).astype(jnp.bfloat16)
    pivot_rows = P_SIZE // pan_count
    part = (-lax.dot_general(scaled, cross, contract, preferred_element_type=jnp.float32)).astype(
        jnp.bfloat16
    )
    shared = scatter_sum(part.reshape(pan_count, pivot_rows, P_SIZE), pan_count)
    own_columns = lax.dynamic_slice_in_dim(inverse_pivot, pan_idx * pivot_rows, pivot_rows, 1)
    triangle = lax.dot_general(
        own_columns, inverse_pivot, contract, preferred_element_type=jnp.float32
    )
    pivot = triangle + shared
    return (cross[None], pivot[None])


def solution(mesh):
    placed = (P("grp", "pan"), P(), P(), P(), P("grp", "pan", None), P("grp", None, None))
    return jax.shard_map(
        per_device,
        mesh=mesh,
        in_specs=placed,
        out_specs=(P("grp", "pan", None), P("grp", "pan", None)),
        check_vma=False,
    )
```

```python
import jax
import jax.numpy as jnp
from jax import lax
from jax.sharding import PartitionSpec as P
from jax.experimental import pallas as pl
from jax.experimental.pallas import tpu as pltpu

BLK = 128
P_SIZE = 768


def _scatter_sum_kernel(n, part_ref, out_ref, buf, send_sem, recv_sem, local_sem):
    me = lax.axis_index("pan")
    grp = lax.axis_index("grp")
    mesh_ids = pl.DeviceIdType.MESH

    barrier = pltpu.get_barrier_semaphore()

    def greet(k, carry):
        peer = lax.rem(me + k, n)
        pl.semaphore_signal(barrier, 1, device_id=(grp, peer), device_id_type=mesh_ids)
        return carry

    lax.fori_loop(1, n, greet, 0)
    pl.semaphore_wait(barrier, n - 1)

    own = pltpu.make_async_copy(part_ref.at[me], buf.at[0], local_sem)
    own.start()

    def send(k):
        peer = lax.rem(me + k, n)
        return pltpu.make_async_remote_copy(
            src_ref=part_ref.at[peer],
            dst_ref=buf.at[k],
            send_sem=send_sem.at[k],
            recv_sem=recv_sem.at[k],
            device_id=(grp, peer),
            device_id_type=mesh_ids,
        )

    def start(k, carry):
        send(k).start()
        return carry

    def finish(k, carry):
        send(k).wait()
        return carry

    lax.fori_loop(1, n, start, 0)
    own.wait()
    lax.fori_loop(1, n, finish, 0)

    out_ref[...] = buf[0].astype(jnp.float32)

    def accumulate(k, carry):
        out_ref[...] += buf[k].astype(jnp.float32)
        return carry

    lax.fori_loop(1, n, accumulate, 0)


def scatter_sum(part, n):
    _, rows, cols = part.shape
    return pl.pallas_call(
        lambda *refs: _scatter_sum_kernel(n, *refs),
        out_shape=jax.ShapeDtypeStruct((rows, cols), jnp.float32),
        in_specs=[pl.BlockSpec(memory_space=pl.ANY)],
        out_specs=pl.BlockSpec(memory_space=pltpu.VMEM),
        scratch_shapes=[
            pltpu.VMEM((n, rows, cols), part.dtype),
            pltpu.SemaphoreType.DMA((n,)),
            pltpu.SemaphoreType.DMA((n,)),
            pltpu.SemaphoreType.DMA,
        ],
        compiler_params=pltpu.CompilerParams(collective_id=0, has_side_effects=True),
    )(part)


def per_device(anc_rows, row_home, block_lists, front_blocks, panel, pivot_inverse):
    groups = lax.axis_size("grp")
    pan_count = lax.axis_size("pan")
    group_idx = lax.axis_index("grp")
    pan_idx = lax.axis_index("pan")
    block_count = row_home.shape[0]
    front_len = block_lists.shape[1]
    rb_local = front_len // pan_count
    cb_local = anc_rows.shape[1] // BLK
    stored_blocks = anc_rows.shape[0] // BLK
    windows = block_count // cb_local
    win_per_group = windows // groups
    per_src = win_per_group * rb_local
    contract = (((0,), (0,)), ((), ()))

    home_of_window = row_home[cb_local * jnp.arange(windows, dtype=jnp.int32)] // stored_blocks
    win = jnp.argsort(home_of_window * windows + jnp.arange(windows, dtype=jnp.int32))
    win = win.reshape(groups, win_per_group).astype(jnp.int32)
    pos = (rb_local * win[:, :, None] + jnp.arange(rb_local, dtype=jnp.int32)).reshape(
        groups, per_src
    )

    my_pos = lax.dynamic_index_in_dim(pos, group_idx, 0, keepdims=False)
    row_blocks = jnp.take(block_lists, my_pos, axis=1)
    slots = jnp.take(row_home, row_blocks) - stored_blocks * group_idx
    cols = lax.dynamic_slice_in_dim(block_lists, rb_local * pan_idx, rb_local, axis=1) - (
        cb_local * pan_idx
    )
    local = anc_rows.reshape(stored_blocks, BLK, cb_local, BLK)
    outgoing = local[slots[:, :, None], :, cols[:, None, :], :]
    received = lax.all_to_all(outgoing, "grp", split_axis=0, concat_axis=0, tiled=True)
    order = jnp.argsort(pos.reshape(groups * per_src)).astype(jnp.int32)
    sigma = jnp.take(received.reshape(groups * per_src, rb_local, BLK, BLK), order, axis=0)

    my_blocks = pan_idx * rb_local + jnp.arange(rb_local, dtype=jnp.int32)
    front_live = lax.dynamic_index_in_dim(front_blocks, group_idx, 0, keepdims=False)
    alive_rows = jnp.repeat(my_blocks < front_live, BLK)
    inverse_pivot = pivot_inverse[0]
    scaled = jnp.dot(panel[0], inverse_pivot, preferred_element_type=jnp.float32)
    scaled = jnp.where(alive_rows[:, None], scaled, jnp.zeros_like(scaled)).astype(jnp.bfloat16)
    full = lax.all_gather(scaled, "pan", axis=0, tiled=True)
    product = lax.dot_general(
        sigma,
        full.reshape(front_len, BLK, P_SIZE),
        (((0, 2), (0, 1)), ((), ())),
        preferred_element_type=jnp.float32,
    ).reshape(rb_local * BLK, P_SIZE)
    cross = jnp.where(alive_rows[:, None], -product, jnp.zeros_like(product)).astype(jnp.bfloat16)
    pivot_rows = P_SIZE // pan_count
    part = (-lax.dot_general(scaled, cross, contract, preferred_element_type=jnp.float32)).astype(
        jnp.bfloat16
    )
    pieces = lax.all_to_all(
        part.reshape(pan_count, pivot_rows, P_SIZE), "pan", split_axis=0, concat_axis=0, tiled=True
    )
    shared = jnp.sum(pieces.astype(jnp.float32), axis=0)
    own_columns = lax.dynamic_slice_in_dim(inverse_pivot, pan_idx * pivot_rows, pivot_rows, 1)
    triangle = lax.dot_general(
        own_columns, inverse_pivot, contract, preferred_element_type=jnp.float32
    )
    pivot = triangle + shared
    return (cross[None], pivot[None])


def solution(mesh):
    placed = (P("grp", "pan"), P(), P(), P(), P("grp", "pan", None), P("grp", None, None))
    return jax.shard_map(
        per_device,
        mesh=mesh,
        in_specs=placed,
        out_specs=(P("grp", "pan", None), P("grp", "pan", None)),
        check_vma=False,
    )
```

```python
import functools

import jax
import jax.numpy as jnp
from jax import lax
from jax.sharding import PartitionSpec as P
from jax.experimental import pallas as pl
from jax.experimental.pallas import tpu as pltpu

BLK = 128
P_SIZE = 768
SPREAD_COLS = 256


def _scatter_sum_kernel(n, part_ref, out_ref, buf, send_sem, recv_sem, local_sem):
    me = lax.axis_index("pan")
    grp = lax.axis_index("grp")
    mesh_ids = pl.DeviceIdType.MESH

    barrier = pltpu.get_barrier_semaphore()

    def greet(k, carry):
        peer = lax.rem(me + k, n)
        pl.semaphore_signal(barrier, 1, device_id=(grp, peer), device_id_type=mesh_ids)
        return carry

    lax.fori_loop(1, n, greet, 0)
    pl.semaphore_wait(barrier, n - 1)

    own = pltpu.make_async_copy(part_ref.at[me], buf.at[0], local_sem)
    own.start()

    def send(k):
        peer = lax.rem(me + k, n)
        return pltpu.make_async_remote_copy(
            src_ref=part_ref.at[peer],
            dst_ref=buf.at[k],
            send_sem=send_sem.at[k],
            recv_sem=recv_sem.at[k],
            device_id=(grp, peer),
            device_id_type=mesh_ids,
        )

    def start(k, carry):
        send(k).start()
        return carry

    def finish(k, carry):
        send(k).wait()
        return carry

    lax.fori_loop(1, n, start, 0)
    own.wait()
    lax.fori_loop(1, n, finish, 0)

    out_ref[...] = buf[0].astype(jnp.float32)

    def accumulate(k, carry):
        out_ref[...] += buf[k].astype(jnp.float32)
        return carry

    lax.fori_loop(1, n, accumulate, 0)


def scatter_sum(part, n):
    _, rows, cols = part.shape
    return pl.pallas_call(
        lambda *refs: _scatter_sum_kernel(n, *refs),
        out_shape=jax.ShapeDtypeStruct((rows, cols), jnp.float32),
        in_specs=[pl.BlockSpec(memory_space=pl.ANY)],
        out_specs=pl.BlockSpec(memory_space=pltpu.VMEM),
        scratch_shapes=[
            pltpu.VMEM((n, rows, cols), part.dtype),
            pltpu.SemaphoreType.DMA((n,)),
            pltpu.SemaphoreType.DMA((n,)),
            pltpu.SemaphoreType.DMA,
        ],
        compiler_params=pltpu.CompilerParams(collective_id=0, has_side_effects=True),
    )(part)


def _spread_kernel(n, block_ref, out_ref, send_sem, recv_sem, local_sem):
    me = lax.axis_index("pan")
    grp = lax.axis_index("grp")
    mesh_ids = pl.DeviceIdType.MESH

    barrier = pltpu.get_barrier_semaphore()

    def greet(k, carry):
        peer = lax.rem(me + k, n)
        pl.semaphore_signal(barrier, 1, device_id=(grp, peer), device_id_type=mesh_ids)
        return carry

    lax.fori_loop(1, n, greet, 0)
    pl.semaphore_wait(barrier, n - 1)

    own = pltpu.make_async_copy(block_ref, out_ref.at[0], local_sem)
    own.start()

    def send(k):
        peer = lax.rem(me + k, n)
        return pltpu.make_async_remote_copy(
            src_ref=block_ref,
            dst_ref=out_ref.at[k],
            send_sem=send_sem.at[k],
            recv_sem=recv_sem.at[k],
            device_id=(grp, peer),
            device_id_type=mesh_ids,
        )

    def start(k, carry):
        send(k).start()
        return carry

    def finish(k, carry):
        send(k).wait()
        return carry

    lax.fori_loop(1, n, start, 0)
    own.wait()
    lax.fori_loop(1, n, finish, 0)


def spread(block, n):
    rows, cols = block.shape
    return pl.pallas_call(
        functools.partial(_spread_kernel, n),
        out_shape=jax.ShapeDtypeStruct((n, rows, cols), block.dtype),
        in_specs=[pl.BlockSpec(memory_space=pl.ANY)],
        out_specs=pl.BlockSpec(memory_space=pl.ANY),
        scratch_shapes=[
            pltpu.SemaphoreType.DMA((n,)),
            pltpu.SemaphoreType.DMA((n,)),
            pltpu.SemaphoreType.DMA,
        ],
        compiler_params=pltpu.CompilerParams(collective_id=1, has_side_effects=True),
        cost_estimate=pl.CostEstimate(
            flops=0, bytes_accessed=2 * n * rows * cols * block.dtype.itemsize, transcendentals=0
        ),
    )(block)


def per_device(anc_rows, row_home, block_lists, front_blocks, panel, pivot_inverse):
    groups = lax.axis_size("grp")
    pan_count = lax.axis_size("pan")
    group_idx = lax.axis_index("grp")
    pan_idx = lax.axis_index("pan")
    block_count = row_home.shape[0]
    front_len = block_lists.shape[1]
    rb_local = front_len // pan_count
    cb_local = anc_rows.shape[1] // BLK
    stored_blocks = anc_rows.shape[0] // BLK
    windows = block_count // cb_local
    win_per_group = windows // groups
    per_src = win_per_group * rb_local
    contract = (((0,), (0,)), ((), ()))

    home_of_window = row_home[cb_local * jnp.arange(windows, dtype=jnp.int32)] // stored_blocks
    win = jnp.argsort(home_of_window * windows + jnp.arange(windows, dtype=jnp.int32))
    win = win.reshape(groups, win_per_group).astype(jnp.int32)
    pos = (rb_local * win[:, :, None] + jnp.arange(rb_local, dtype=jnp.int32)).reshape(
        groups, per_src
    )

    my_pos = lax.dynamic_index_in_dim(pos, group_idx, 0, keepdims=False)
    row_blocks = jnp.take(block_lists, my_pos, axis=1)
    slots = jnp.take(row_home, row_blocks) - stored_blocks * group_idx
    cols = lax.dynamic_slice_in_dim(block_lists, rb_local * pan_idx, rb_local, axis=1) - (
        cb_local * pan_idx
    )
    local = anc_rows.reshape(stored_blocks, BLK, cb_local, BLK)
    outgoing = local[slots[:, :, None], :, cols[:, None, :], :]
    received = lax.all_to_all(outgoing, "grp", split_axis=0, concat_axis=0, tiled=True)
    order = jnp.argsort(pos.reshape(groups * per_src)).astype(jnp.int32)
    sigma = jnp.take(received.reshape(groups * per_src, rb_local, BLK, BLK), order, axis=0)

    my_blocks = pan_idx * rb_local + jnp.arange(rb_local, dtype=jnp.int32)
    front_live = lax.dynamic_index_in_dim(front_blocks, group_idx, 0, keepdims=False)
    alive_rows = jnp.repeat(my_blocks < front_live, BLK)
    inverse_pivot = pivot_inverse[0]
    scaled = jnp.dot(panel[0], inverse_pivot, preferred_element_type=jnp.float32)
    scaled = jnp.where(alive_rows[:, None], scaled, jnp.zeros_like(scaled)).astype(jnp.bfloat16)
    gathered = P_SIZE - SPREAD_COLS
    full = lax.all_gather(scaled[:, :gathered], "pan", axis=0, tiled=True)
    near = lax.dot_general(
        sigma,
        full.reshape(front_len, BLK, gathered),
        (((0, 2), (0, 1)), ((), ())),
        preferred_element_type=jnp.float32,
    ).reshape(rb_local * BLK, gathered)
    slots = spread(scaled[:, gathered:], pan_count)
    source = lax.rem(pan_idx - jnp.arange(pan_count, dtype=jnp.int32) + pan_count, pan_count)
    sigma_by_slot = jnp.take(
        sigma.reshape(pan_count, rb_local, rb_local, BLK, BLK), source, axis=0
    )
    far = lax.dot_general(
        sigma_by_slot,
        slots.reshape(pan_count, rb_local, BLK, SPREAD_COLS),
        (((0, 1, 3), (0, 1, 2)), ((), ())),
        preferred_element_type=jnp.float32,
    ).reshape(rb_local * BLK, SPREAD_COLS)
    product = jnp.concatenate([near, far], axis=1)
    cross = jnp.where(alive_rows[:, None], -product, jnp.zeros_like(product)).astype(jnp.bfloat16)
    pivot_rows = P_SIZE // pan_count
    part = (-lax.dot_general(scaled, cross, contract, preferred_element_type=jnp.float32)).astype(
        jnp.bfloat16
    )
    shared = scatter_sum(part.reshape(pan_count, pivot_rows, P_SIZE), pan_count)
    own_columns = lax.dynamic_slice_in_dim(inverse_pivot, pan_idx * pivot_rows, pivot_rows, 1)
    triangle = lax.dot_general(
        own_columns, inverse_pivot, contract, preferred_element_type=jnp.float32
    )
    pivot = triangle + shared
    return (cross[None], pivot[None])


def solution(mesh):
    placed = (P("grp", "pan"), P(), P(), P(), P("grp", "pan", None), P("grp", None, None))
    return jax.shard_map(
        per_device,
        mesh=mesh,
        in_specs=placed,
        out_specs=(P("grp", "pan", None), P("grp", "pan", None)),
        check_vma=False,
    )
```

```python
import jax
import jax.numpy as jnp
from jax import lax
from jax.sharding import PartitionSpec as P
from jax.experimental import pallas as pl
from jax.experimental.pallas import tpu as pltpu

BLK = 128
P_SIZE = 768


def _scatter_sum_kernel(n, part_ref, out_ref, buf, send_sem, recv_sem, local_sem):
    me = lax.axis_index("pan")
    grp = lax.axis_index("grp")
    mesh_ids = pl.DeviceIdType.MESH

    barrier = pltpu.get_barrier_semaphore()

    def greet(k, carry):
        peer = lax.rem(me + k, n)
        pl.semaphore_signal(barrier, 1, device_id=(grp, peer), device_id_type=mesh_ids)
        return carry

    lax.fori_loop(1, n, greet, 0)
    pl.semaphore_wait(barrier, n - 1)

    own = pltpu.make_async_copy(part_ref.at[me], buf.at[0], local_sem)
    own.start()

    def send(k):
        peer = lax.rem(me + k, n)
        return pltpu.make_async_remote_copy(
            src_ref=part_ref.at[peer],
            dst_ref=buf.at[k],
            send_sem=send_sem.at[k],
            recv_sem=recv_sem.at[k],
            device_id=(grp, peer),
            device_id_type=mesh_ids,
        )

    def start(k, carry):
        send(k).start()
        return carry

    def finish(k, carry):
        send(k).wait()
        return carry

    lax.fori_loop(1, n, start, 0)
    own.wait()
    lax.fori_loop(1, n, finish, 0)

    out_ref[...] = buf[0].astype(jnp.float32)

    def accumulate(k, carry):
        out_ref[...] += buf[k].astype(jnp.float32)
        return carry

    lax.fori_loop(1, n, accumulate, 0)


def scatter_sum(part, n):
    _, rows, cols = part.shape
    return pl.pallas_call(
        lambda *refs: _scatter_sum_kernel(n, *refs),
        out_shape=jax.ShapeDtypeStruct((rows, cols), jnp.float32),
        in_specs=[pl.BlockSpec(memory_space=pltpu.VMEM)],
        out_specs=pl.BlockSpec(memory_space=pltpu.VMEM),
        scratch_shapes=[
            pltpu.VMEM((n, rows, cols), part.dtype),
            pltpu.SemaphoreType.DMA((n,)),
            pltpu.SemaphoreType.DMA((n,)),
            pltpu.SemaphoreType.DMA,
        ],
        compiler_params=pltpu.CompilerParams(collective_id=0, has_side_effects=True),
    )(part)


def per_device(anc_rows, row_home, block_lists, front_blocks, panel, pivot_inverse):
    groups = lax.axis_size("grp")
    pan_count = lax.axis_size("pan")
    group_idx = lax.axis_index("grp")
    pan_idx = lax.axis_index("pan")
    block_count = row_home.shape[0]
    front_len = block_lists.shape[1]
    rb_local = front_len // pan_count
    cb_local = anc_rows.shape[1] // BLK
    stored_blocks = anc_rows.shape[0] // BLK
    windows = block_count // cb_local
    win_per_group = windows // groups
    per_src = win_per_group * rb_local
    contract = (((0,), (0,)), ((), ()))

    home_of_window = row_home[cb_local * jnp.arange(windows, dtype=jnp.int32)] // stored_blocks
    win = jnp.argsort(home_of_window * windows + jnp.arange(windows, dtype=jnp.int32))
    win = win.reshape(groups, win_per_group).astype(jnp.int32)
    pos = (rb_local * win[:, :, None] + jnp.arange(rb_local, dtype=jnp.int32)).reshape(
        groups, per_src
    )

    my_pos = lax.dynamic_index_in_dim(pos, group_idx, 0, keepdims=False)
    row_blocks = jnp.take(block_lists, my_pos, axis=1)
    slots = jnp.take(row_home, row_blocks) - stored_blocks * group_idx
    cols = lax.dynamic_slice_in_dim(block_lists, rb_local * pan_idx, rb_local, axis=1) - (
        cb_local * pan_idx
    )
    local = anc_rows.reshape(stored_blocks, BLK, cb_local, BLK)
    outgoing = local[slots[:, :, None], :, cols[:, None, :], :]
    received = lax.all_to_all(outgoing, "grp", split_axis=0, concat_axis=0, tiled=True)
    order = jnp.argsort(pos.reshape(groups * per_src)).astype(jnp.int32)
    sigma = jnp.take(received.reshape(groups * per_src, rb_local, BLK, BLK), order, axis=0)

    my_blocks = pan_idx * rb_local + jnp.arange(rb_local, dtype=jnp.int32)
    front_live = lax.dynamic_index_in_dim(front_blocks, group_idx, 0, keepdims=False)
    alive_rows = jnp.repeat(my_blocks < front_live, BLK)
    inverse_pivot = pivot_inverse[0]
    scaled = jnp.dot(panel[0], inverse_pivot, preferred_element_type=jnp.float32)
    scaled = jnp.where(alive_rows[:, None], scaled, jnp.zeros_like(scaled)).astype(jnp.bfloat16)
    full = lax.all_gather(scaled, "pan", axis=0, tiled=True)
    product = lax.dot_general(
        sigma,
        full.reshape(front_len, BLK, P_SIZE),
        (((0, 2), (0, 1)), ((), ())),
        preferred_element_type=jnp.float32,
    ).reshape(rb_local * BLK, P_SIZE)
    cross = jnp.where(alive_rows[:, None], -product, jnp.zeros_like(product)).astype(jnp.bfloat16)
    pivot_rows = P_SIZE // pan_count
    part = (-lax.dot_general(scaled, cross, contract, preferred_element_type=jnp.float32)).astype(
        jnp.bfloat16
    )
    shared = scatter_sum(part.reshape(pan_count, pivot_rows, P_SIZE), pan_count)
    own_columns = lax.dynamic_slice_in_dim(inverse_pivot, pan_idx * pivot_rows, pivot_rows, 1)
    triangle = lax.dot_general(
        own_columns, inverse_pivot, contract, preferred_element_type=jnp.float32
    )
    pivot = triangle + shared
    return (cross[None], pivot[None])


def solution(mesh):
    placed = (P("grp", "pan"), P(), P(), P(), P("grp", "pan", None), P("grp", None, None))
    return jax.shard_map(
        per_device,
        mesh=mesh,
        in_specs=placed,
        out_specs=(P("grp", "pan", None), P("grp", "pan", None)),
        check_vma=False,
    )
```

```python
import functools

import jax
import jax.numpy as jnp
from jax import lax
from jax.sharding import PartitionSpec as P
from jax.experimental import pallas as pl
from jax.experimental.pallas import tpu as pltpu

BLK = 128
P_SIZE = 768


def _scatter_sum_kernel(n, part_ref, out_ref, buf, send_sem, recv_sem, local_sem):
    me = lax.axis_index("pan")
    grp = lax.axis_index("grp")
    mesh_ids = pl.DeviceIdType.MESH

    barrier = pltpu.get_barrier_semaphore()

    def greet(k, carry):
        peer = lax.rem(me + k, n)
        pl.semaphore_signal(barrier, 1, device_id=(grp, peer), device_id_type=mesh_ids)
        return carry

    lax.fori_loop(1, n, greet, 0)
    pl.semaphore_wait(barrier, n - 1)

    own = pltpu.make_async_copy(part_ref.at[me], buf.at[0], local_sem)
    own.start()

    def send(k):
        peer = lax.rem(me + k, n)
        return pltpu.make_async_remote_copy(
            src_ref=part_ref.at[peer],
            dst_ref=buf.at[k],
            send_sem=send_sem.at[k],
            recv_sem=recv_sem.at[k],
            device_id=(grp, peer),
            device_id_type=mesh_ids,
        )

    def start(k, carry):
        send(k).start()
        return carry

    def finish(k, carry):
        send(k).wait()
        return carry

    lax.fori_loop(1, n, start, 0)
    own.wait()
    lax.fori_loop(1, n, finish, 0)

    out_ref[...] = buf[0].astype(jnp.float32)

    def accumulate(k, carry):
        out_ref[...] += buf[k].astype(jnp.float32)
        return carry

    lax.fori_loop(1, n, accumulate, 0)


def scatter_sum(part, n):
    _, rows, cols = part.shape
    return pl.pallas_call(
        lambda *refs: _scatter_sum_kernel(n, *refs),
        out_shape=jax.ShapeDtypeStruct((rows, cols), jnp.float32),
        in_specs=[pl.BlockSpec(memory_space=pl.ANY)],
        out_specs=pl.BlockSpec(memory_space=pltpu.VMEM),
        scratch_shapes=[
            pltpu.VMEM((n, rows, cols), part.dtype),
            pltpu.SemaphoreType.DMA((n,)),
            pltpu.SemaphoreType.DMA((n,)),
            pltpu.SemaphoreType.DMA,
        ],
        compiler_params=pltpu.CompilerParams(collective_id=0, has_side_effects=True),
    )(part)


CHUNKS = 4


def _tail_kernel(
    n, sigma_ref, full_ref, scaled_ref, keep_ref, cross_ref, out_ref,
    sig_v, full_v, acc, part_v, buf, load_sem, send_sem, recv_sem, local_sem,
):
    me = lax.axis_index("pan")
    grp = lax.axis_index("grp")
    mesh_ids = pl.DeviceIdType.MESH
    blocks = sig_v.shape[0]
    per_chunk = blocks // CHUNKS
    rows = part_v.shape[1]

    barrier = pltpu.get_barrier_semaphore()

    def greet(k, carry):
        peer = lax.rem(me + k, n)
        pl.semaphore_signal(barrier, 1, device_id=(grp, peer), device_id_type=mesh_ids)
        return carry

    lax.fori_loop(1, n, greet, 0)

    def loads(c):
        span = pl.ds(c * per_chunk, per_chunk)
        return (
            pltpu.make_async_copy(sigma_ref.at[span], sig_v.at[span], load_sem.at[0, c]),
            pltpu.make_async_copy(full_ref.at[span], full_v.at[span], load_sem.at[1, c]),
        )

    for c in range(CHUNKS):
        for copy in loads(c):
            copy.start()

    acc[...] = jnp.zeros_like(acc)
    contract = (((0,), (0,)), ((), ()))
    for c in range(CHUNKS):
        for copy in loads(c):
            copy.wait()

        def step(j, carry):
            block = full_v[j]
            for u in range(acc.shape[0]):
                acc[u] += lax.dot_general(
                    sig_v[j, u], block, contract, preferred_element_type=jnp.float32
                )
            return carry

        lax.fori_loop(c * per_chunk, (c + 1) * per_chunk, step, 0)

    width = acc.shape[2]
    total = acc[...].reshape(acc.shape[0] * acc.shape[1], width)
    cross = jnp.where(keep_ref[...] > 0, -total, jnp.zeros_like(total)).astype(cross_ref.dtype)
    cross_ref[...] = cross
    part = -lax.dot_general(scaled_ref[...], cross, contract, preferred_element_type=jnp.float32)
    for k in range(n):
        part_v[k] = part[k * rows : (k + 1) * rows]

    pl.semaphore_wait(barrier, n - 1)

    own = pltpu.make_async_copy(part_v.at[me], buf.at[0], local_sem)
    own.start()

    def send(k):
        peer = lax.rem(me + k, n)
        return pltpu.make_async_remote_copy(
            src_ref=part_v.at[peer],
            dst_ref=buf.at[k],
            send_sem=send_sem.at[k],
            recv_sem=recv_sem.at[k],
            device_id=(grp, peer),
            device_id_type=mesh_ids,
        )

    def start(k, carry):
        send(k).start()
        return carry

    def finish(k, carry):
        send(k).wait()
        return carry

    lax.fori_loop(1, n, start, 0)
    own.wait()
    lax.fori_loop(1, n, finish, 0)

    out_ref[...] = buf[0]

    def accumulate(k, carry):
        out_ref[...] += buf[k]
        return carry

    lax.fori_loop(1, n, accumulate, 0)


def cross_and_pivot_sum(sigma, full, scaled, keep, n):
    blocks, halves, _, _ = sigma.shape
    width = full.shape[1]
    out_rows = halves * BLK
    rows = width // n
    full = full.reshape(blocks, BLK, width)
    return pl.pallas_call(
        functools.partial(_tail_kernel, n),
        out_shape=(
            jax.ShapeDtypeStruct((out_rows, width), jnp.bfloat16),
            jax.ShapeDtypeStruct((rows, width), jnp.float32),
        ),
        in_specs=[
            pl.BlockSpec(memory_space=pl.ANY),
            pl.BlockSpec(memory_space=pl.ANY),
            pl.BlockSpec(memory_space=pltpu.VMEM),
            pl.BlockSpec(memory_space=pltpu.VMEM),
        ],
        out_specs=(
            pl.BlockSpec(memory_space=pltpu.VMEM),
            pl.BlockSpec(memory_space=pltpu.VMEM),
        ),
        scratch_shapes=[
            pltpu.VMEM(sigma.shape, sigma.dtype),
            pltpu.VMEM(full.shape, full.dtype),
            pltpu.VMEM((halves, BLK, width), jnp.float32),
            pltpu.VMEM((n, rows, width), jnp.float32),
            pltpu.VMEM((n, rows, width), jnp.float32),
            pltpu.SemaphoreType.DMA((2, CHUNKS)),
            pltpu.SemaphoreType.DMA((n,)),
            pltpu.SemaphoreType.DMA((n,)),
            pltpu.SemaphoreType.DMA,
        ],
        compiler_params=pltpu.CompilerParams(
            collective_id=0, has_side_effects=True, vmem_limit_bytes=60 * 1024 * 1024
        ),
        cost_estimate=pl.CostEstimate(
            flops=2 * out_rows * blocks * BLK * width + 2 * width * out_rows * width,
            bytes_accessed=sigma.size * 2 + full.size * 2 + 2 * n * rows * width * 4,
            transcendentals=0,
        ),
    )(sigma, full, scaled, keep)


def per_device(anc_rows, row_home, block_lists, front_blocks, panel, pivot_inverse):
    groups = lax.axis_size("grp")
    pan_count = lax.axis_size("pan")
    group_idx = lax.axis_index("grp")
    pan_idx = lax.axis_index("pan")
    block_count = row_home.shape[0]
    front_len = block_lists.shape[1]
    rb_local = front_len // pan_count
    cb_local = anc_rows.shape[1] // BLK
    stored_blocks = anc_rows.shape[0] // BLK
    windows = block_count // cb_local
    win_per_group = windows // groups
    per_src = win_per_group * rb_local
    contract = (((0,), (0,)), ((), ()))

    home_of_window = row_home[cb_local * jnp.arange(windows, dtype=jnp.int32)] // stored_blocks
    win = jnp.argsort(home_of_window * windows + jnp.arange(windows, dtype=jnp.int32))
    win = win.reshape(groups, win_per_group).astype(jnp.int32)
    pos = (rb_local * win[:, :, None] + jnp.arange(rb_local, dtype=jnp.int32)).reshape(
        groups, per_src
    )

    my_pos = lax.dynamic_index_in_dim(pos, group_idx, 0, keepdims=False)
    row_blocks = jnp.take(block_lists, my_pos, axis=1)
    slots = jnp.take(row_home, row_blocks) - stored_blocks * group_idx
    cols = lax.dynamic_slice_in_dim(block_lists, rb_local * pan_idx, rb_local, axis=1) - (
        cb_local * pan_idx
    )
    local = anc_rows.reshape(stored_blocks, BLK, cb_local, BLK)
    outgoing = local[slots[:, :, None], :, cols[:, None, :], :]
    received = lax.all_to_all(outgoing, "grp", split_axis=0, concat_axis=0, tiled=True)
    order = jnp.argsort(pos.reshape(groups * per_src)).astype(jnp.int32)
    sigma = jnp.take(received.reshape(groups * per_src, rb_local, BLK, BLK), order, axis=0)

    my_blocks = pan_idx * rb_local + jnp.arange(rb_local, dtype=jnp.int32)
    front_live = lax.dynamic_index_in_dim(front_blocks, group_idx, 0, keepdims=False)
    alive_rows = jnp.repeat(my_blocks < front_live, BLK)
    inverse_pivot = pivot_inverse[0]
    scaled = jnp.dot(panel[0], inverse_pivot, preferred_element_type=jnp.float32)
    scaled = jnp.where(alive_rows[:, None], scaled, jnp.zeros_like(scaled)).astype(jnp.bfloat16)
    full = lax.all_gather(scaled, "pan", axis=0, tiled=True)
    pivot_rows = P_SIZE // pan_count
    keep = alive_rows[:, None].astype(jnp.float32)
    cross, shared = cross_and_pivot_sum(sigma, full, scaled, keep, pan_count)
    own_columns = lax.dynamic_slice_in_dim(inverse_pivot, pan_idx * pivot_rows, pivot_rows, 1)
    triangle = lax.dot_general(
        own_columns, inverse_pivot, contract, preferred_element_type=jnp.float32
    )
    pivot = triangle + shared
    return (cross[None], pivot[None])


def solution(mesh):
    placed = (P("grp", "pan"), P(), P(), P(), P("grp", "pan", None), P("grp", None, None))
    return jax.shard_map(
        per_device,
        mesh=mesh,
        in_specs=placed,
        out_specs=(P("grp", "pan", None), P("grp", "pan", None)),
        check_vma=False,
    )
```

```python
import functools

import jax
import jax.numpy as jnp
from jax import lax
from jax.sharding import PartitionSpec as P
from jax.experimental import pallas as pl
from jax.experimental.pallas import tpu as pltpu

BLK = 128
P_SIZE = 768


def _scatter_sum_kernel(n, part_ref, out_ref, buf, send_sem, recv_sem, local_sem):
    me = lax.axis_index("pan")
    grp = lax.axis_index("grp")
    mesh_ids = pl.DeviceIdType.MESH

    barrier = pltpu.get_barrier_semaphore()

    def greet(k, carry):
        peer = lax.rem(me + k, n)
        pl.semaphore_signal(barrier, 1, device_id=(grp, peer), device_id_type=mesh_ids)
        return carry

    lax.fori_loop(1, n, greet, 0)
    pl.semaphore_wait(barrier, n - 1)

    own = pltpu.make_async_copy(part_ref.at[me], buf.at[0], local_sem)
    own.start()

    def send(k):
        peer = lax.rem(me + k, n)
        return pltpu.make_async_remote_copy(
            src_ref=part_ref.at[peer],
            dst_ref=buf.at[k],
            send_sem=send_sem.at[k],
            recv_sem=recv_sem.at[k],
            device_id=(grp, peer),
            device_id_type=mesh_ids,
        )

    def start(k, carry):
        send(k).start()
        return carry

    def finish(k, carry):
        send(k).wait()
        return carry

    lax.fori_loop(1, n, start, 0)
    own.wait()
    lax.fori_loop(1, n, finish, 0)

    out_ref[...] = buf[0].astype(jnp.float32)

    def accumulate(k, carry):
        out_ref[...] += buf[k].astype(jnp.float32)
        return carry

    lax.fori_loop(1, n, accumulate, 0)


def scatter_sum(part, n):
    _, rows, cols = part.shape
    return pl.pallas_call(
        lambda *refs: _scatter_sum_kernel(n, *refs),
        out_shape=jax.ShapeDtypeStruct((rows, cols), jnp.float32),
        in_specs=[pl.BlockSpec(memory_space=pl.ANY)],
        out_specs=pl.BlockSpec(memory_space=pltpu.VMEM),
        scratch_shapes=[
            pltpu.VMEM((n, rows, cols), part.dtype),
            pltpu.SemaphoreType.DMA((n,)),
            pltpu.SemaphoreType.DMA((n,)),
            pltpu.SemaphoreType.DMA,
        ],
        compiler_params=pltpu.CompilerParams(collective_id=0, has_side_effects=True),
    )(part)


CHUNKS = 4


def _tail_kernel(
    n, sigma_ref, full_ref, scaled_ref, keep_ref, cross_ref, out_ref,
    sig_v, full_v, acc, part_v, buf, load_sem, send_sem, recv_sem, local_sem,
):
    me = lax.axis_index("pan")
    grp = lax.axis_index("grp")
    mesh_ids = pl.DeviceIdType.MESH
    per_chunk = full_v.shape[0] // CHUNKS
    rows = part_v.shape[1]

    barrier = pltpu.get_barrier_semaphore()

    def greet(k, carry):
        peer = lax.rem(me + k, n)
        pl.semaphore_signal(barrier, 1, device_id=(grp, peer), device_id_type=mesh_ids)
        return carry

    lax.fori_loop(1, n, greet, 0)

    def loads(c):
        span = pl.ds(c * per_chunk, per_chunk)
        return (
            pltpu.make_async_copy(sigma_ref.at[c], sig_v.at[c], load_sem.at[0, c]),
            pltpu.make_async_copy(full_ref.at[span], full_v.at[span], load_sem.at[1, c]),
        )

    for c in range(CHUNKS):
        for copy in loads(c):
            copy.start()

    acc[...] = jnp.zeros_like(acc)
    contract = (((0,), (0,)), ((), ()))
    for c in range(CHUNKS):
        for copy in loads(c):
            copy.wait()
        acc[...] += jnp.dot(
            sig_v[c], full_v[pl.ds(c * per_chunk, per_chunk)], preferred_element_type=jnp.float32
        )

    total = acc[...]
    cross = jnp.where(keep_ref[...] > 0, -total, jnp.zeros_like(total)).astype(cross_ref.dtype)
    cross_ref[...] = cross
    part = -lax.dot_general(scaled_ref[...], cross, contract, preferred_element_type=jnp.float32)
    for k in range(n):
        part_v[k] = part[k * rows : (k + 1) * rows]

    pl.semaphore_wait(barrier, n - 1)

    own = pltpu.make_async_copy(part_v.at[me], buf.at[0], local_sem)
    own.start()

    def send(k):
        peer = lax.rem(me + k, n)
        return pltpu.make_async_remote_copy(
            src_ref=part_v.at[peer],
            dst_ref=buf.at[k],
            send_sem=send_sem.at[k],
            recv_sem=recv_sem.at[k],
            device_id=(grp, peer),
            device_id_type=mesh_ids,
        )

    def start(k, carry):
        send(k).start()
        return carry

    def finish(k, carry):
        send(k).wait()
        return carry

    lax.fori_loop(1, n, start, 0)
    own.wait()
    lax.fori_loop(1, n, finish, 0)

    out_ref[...] = buf[0]

    def accumulate(k, carry):
        out_ref[...] += buf[k]
        return carry

    lax.fori_loop(1, n, accumulate, 0)


def cross_and_pivot_sum(sigma, full, scaled, keep, n):
    blocks, halves, _, _ = sigma.shape
    width = full.shape[1]
    out_rows = halves * BLK
    rows = width // n
    depth = blocks * BLK // CHUNKS
    sigma = jnp.transpose(sigma, (1, 3, 0, 2)).reshape(out_rows, CHUNKS, depth)
    sigma = jnp.transpose(sigma, (1, 0, 2))
    return pl.pallas_call(
        functools.partial(_tail_kernel, n),
        out_shape=(
            jax.ShapeDtypeStruct((out_rows, width), jnp.bfloat16),
            jax.ShapeDtypeStruct((rows, width), jnp.float32),
        ),
        in_specs=[
            pl.BlockSpec(memory_space=pl.ANY),
            pl.BlockSpec(memory_space=pl.ANY),
            pl.BlockSpec(memory_space=pltpu.VMEM),
            pl.BlockSpec(memory_space=pltpu.VMEM),
        ],
        out_specs=(
            pl.BlockSpec(memory_space=pltpu.VMEM),
            pl.BlockSpec(memory_space=pltpu.VMEM),
        ),
        scratch_shapes=[
            pltpu.VMEM(sigma.shape, sigma.dtype),
            pltpu.VMEM(full.shape, full.dtype),
            pltpu.VMEM((out_rows, width), jnp.float32),
            pltpu.VMEM((n, rows, width), jnp.float32),
            pltpu.VMEM((n, rows, width), jnp.float32),
            pltpu.SemaphoreType.DMA((2, CHUNKS)),
            pltpu.SemaphoreType.DMA((n,)),
            pltpu.SemaphoreType.DMA((n,)),
            pltpu.SemaphoreType.DMA,
        ],
        compiler_params=pltpu.CompilerParams(
            collective_id=0, has_side_effects=True, vmem_limit_bytes=60 * 1024 * 1024
        ),
        cost_estimate=pl.CostEstimate(
            flops=2 * out_rows * blocks * BLK * width + 2 * width * out_rows * width,
            bytes_accessed=sigma.size * 2 + full.size * 2 + 2 * n * rows * width * 4,
            transcendentals=0,
        ),
    )(sigma, full, scaled, keep)


def per_device(anc_rows, row_home, block_lists, front_blocks, panel, pivot_inverse):
    groups = lax.axis_size("grp")
    pan_count = lax.axis_size("pan")
    group_idx = lax.axis_index("grp")
    pan_idx = lax.axis_index("pan")
    block_count = row_home.shape[0]
    front_len = block_lists.shape[1]
    rb_local = front_len // pan_count
    cb_local = anc_rows.shape[1] // BLK
    stored_blocks = anc_rows.shape[0] // BLK
    windows = block_count // cb_local
    win_per_group = windows // groups
    per_src = win_per_group * rb_local
    contract = (((0,), (0,)), ((), ()))

    home_of_window = row_home[cb_local * jnp.arange(windows, dtype=jnp.int32)] // stored_blocks
    win = jnp.argsort(home_of_window * windows + jnp.arange(windows, dtype=jnp.int32))
    win = win.reshape(groups, win_per_group).astype(jnp.int32)
    pos = (rb_local * win[:, :, None] + jnp.arange(rb_local, dtype=jnp.int32)).reshape(
        groups, per_src
    )

    my_pos = lax.dynamic_index_in_dim(pos, group_idx, 0, keepdims=False)
    row_blocks = jnp.take(block_lists, my_pos, axis=1)
    slots = jnp.take(row_home, row_blocks) - stored_blocks * group_idx
    cols = lax.dynamic_slice_in_dim(block_lists, rb_local * pan_idx, rb_local, axis=1) - (
        cb_local * pan_idx
    )
    local = anc_rows.reshape(stored_blocks, BLK, cb_local, BLK)
    outgoing = local[slots[:, :, None], :, cols[:, None, :], :]
    received = lax.all_to_all(outgoing, "grp", split_axis=0, concat_axis=0, tiled=True)
    order = jnp.argsort(pos.reshape(groups * per_src)).astype(jnp.int32)
    sigma = jnp.take(received.reshape(groups * per_src, rb_local, BLK, BLK), order, axis=0)

    my_blocks = pan_idx * rb_local + jnp.arange(rb_local, dtype=jnp.int32)
    front_live = lax.dynamic_index_in_dim(front_blocks, group_idx, 0, keepdims=False)
    alive_rows = jnp.repeat(my_blocks < front_live, BLK)
    inverse_pivot = pivot_inverse[0]
    scaled = jnp.dot(panel[0], inverse_pivot, preferred_element_type=jnp.float32)
    scaled = jnp.where(alive_rows[:, None], scaled, jnp.zeros_like(scaled)).astype(jnp.bfloat16)
    full = lax.all_gather(scaled, "pan", axis=0, tiled=True)
    pivot_rows = P_SIZE // pan_count
    keep = alive_rows[:, None].astype(jnp.float32)
    cross, shared = cross_and_pivot_sum(sigma, full, scaled, keep, pan_count)
    own_columns = lax.dynamic_slice_in_dim(inverse_pivot, pan_idx * pivot_rows, pivot_rows, 1)
    triangle = lax.dot_general(
        own_columns, inverse_pivot, contract, preferred_element_type=jnp.float32
    )
    pivot = triangle + shared
    return (cross[None], pivot[None])


def solution(mesh):
    placed = (P("grp", "pan"), P(), P(), P(), P("grp", "pan", None), P("grp", None, None))
    return jax.shard_map(
        per_device,
        mesh=mesh,
        in_specs=placed,
        out_specs=(P("grp", "pan", None), P("grp", "pan", None)),
        check_vma=False,
    )
```

```python
import functools

import jax
import jax.numpy as jnp
from jax import lax
from jax.sharding import PartitionSpec as P
from jax.experimental import pallas as pl
from jax.experimental.pallas import tpu as pltpu

BLK = 128
P_SIZE = 768


PAN_INNER = 4


def _scatter_sum_kernel(
    inner, outer, part_ref, out_ref, first, mid, second, sems, local_sem
):
    me = lax.axis_index("pan")
    grp = lax.axis_index("grp")
    row, col = me // inner, me % inner
    mesh_ids = pl.DeviceIdType.MESH
    send1, recv1, send2, recv2 = sems

    barrier = pltpu.get_barrier_semaphore()

    def greet_row(k, carry):
        peer = row * inner + lax.rem(col + k, inner)
        pl.semaphore_signal(barrier, 1, device_id=(grp, peer), device_id_type=mesh_ids)
        return carry

    def greet_col(k, carry):
        peer = lax.rem(row + k, outer) * inner + col
        pl.semaphore_signal(barrier, 1, device_id=(grp, peer), device_id_type=mesh_ids)
        return carry

    lax.fori_loop(1, inner, greet_row, 0)
    lax.fori_loop(1, outer, greet_col, 0)
    pl.semaphore_wait(barrier, inner + outer - 2)

    own = pltpu.make_async_copy(part_ref.at[:, col], first.at[0], local_sem)
    own.start()

    def stage_one(k):
        dest = lax.rem(col + k, inner)
        return pltpu.make_async_remote_copy(
            src_ref=part_ref.at[:, dest],
            dst_ref=first.at[k],
            send_sem=send1.at[k],
            recv_sem=recv1.at[k],
            device_id=(grp, row * inner + dest),
            device_id_type=mesh_ids,
        )

    def start_one(k, carry):
        stage_one(k).start()
        return carry

    def finish_one(k, carry):
        stage_one(k).wait()
        return carry

    lax.fori_loop(1, inner, start_one, 0)
    own.wait()
    lax.fori_loop(1, inner, finish_one, 0)

    mid[...] = first[0].astype(jnp.float32)

    def add_first(k, carry):
        mid[...] += first[k].astype(jnp.float32)
        return carry

    lax.fori_loop(1, inner, add_first, 0)

    def stage_two(k):
        dest = lax.rem(row + k, outer)
        return pltpu.make_async_remote_copy(
            src_ref=mid.at[dest],
            dst_ref=second.at[k],
            send_sem=send2.at[k],
            recv_sem=recv2.at[k],
            device_id=(grp, dest * inner + col),
            device_id_type=mesh_ids,
        )

    def start_two(k, carry):
        stage_two(k).start()
        return carry

    def finish_two(k, carry):
        stage_two(k).wait()
        return carry

    lax.fori_loop(1, outer, start_two, 0)
    lax.fori_loop(1, outer, finish_two, 0)

    out_ref[...] = mid[row]

    def add_second(k, carry):
        out_ref[...] += second[k]
        return carry

    lax.fori_loop(1, outer, add_second, 0)


def scatter_sum(part, n):
    _, rows, cols = part.shape
    inner = PAN_INNER
    outer = n // inner
    return pl.pallas_call(
        functools.partial(_scatter_sum_kernel, inner, outer),
        out_shape=jax.ShapeDtypeStruct((rows, cols), jnp.float32),
        in_specs=[pl.BlockSpec(memory_space=pl.ANY)],
        out_specs=pl.BlockSpec(memory_space=pltpu.VMEM),
        scratch_shapes=[
            pltpu.VMEM((inner, outer, rows, cols), part.dtype),
            pltpu.VMEM((outer, rows, cols), jnp.float32),
            pltpu.VMEM((outer, rows, cols), jnp.float32),
            (
                pltpu.SemaphoreType.DMA((inner,)),
                pltpu.SemaphoreType.DMA((inner,)),
                pltpu.SemaphoreType.DMA((outer,)),
                pltpu.SemaphoreType.DMA((outer,)),
            ),
            pltpu.SemaphoreType.DMA,
        ],
        compiler_params=pltpu.CompilerParams(collective_id=0, has_side_effects=True),
    )(part.reshape(outer, inner, rows, cols))


def per_device(anc_rows, row_home, block_lists, front_blocks, panel, pivot_inverse):
    groups = lax.axis_size("grp")
    pan_count = lax.axis_size("pan")
    group_idx = lax.axis_index("grp")
    pan_idx = lax.axis_index("pan")
    block_count = row_home.shape[0]
    front_len = block_lists.shape[1]
    rb_local = front_len // pan_count
    cb_local = anc_rows.shape[1] // BLK
    stored_blocks = anc_rows.shape[0] // BLK
    windows = block_count // cb_local
    win_per_group = windows // groups
    per_src = win_per_group * rb_local
    contract = (((0,), (0,)), ((), ()))

    home_of_window = row_home[cb_local * jnp.arange(windows, dtype=jnp.int32)] // stored_blocks
    win = jnp.argsort(home_of_window * windows + jnp.arange(windows, dtype=jnp.int32))
    win = win.reshape(groups, win_per_group).astype(jnp.int32)
    pos = (rb_local * win[:, :, None] + jnp.arange(rb_local, dtype=jnp.int32)).reshape(
        groups, per_src
    )

    my_pos = lax.dynamic_index_in_dim(pos, group_idx, 0, keepdims=False)
    row_blocks = jnp.take(block_lists, my_pos, axis=1)
    slots = jnp.take(row_home, row_blocks) - stored_blocks * group_idx
    cols = lax.dynamic_slice_in_dim(block_lists, rb_local * pan_idx, rb_local, axis=1) - (
        cb_local * pan_idx
    )
    local = anc_rows.reshape(stored_blocks, BLK, cb_local, BLK)
    outgoing = local[slots[:, :, None], :, cols[:, None, :], :]
    received = lax.all_to_all(outgoing, "grp", split_axis=0, concat_axis=0, tiled=True)
    order = jnp.argsort(pos.reshape(groups * per_src)).astype(jnp.int32)
    sigma = jnp.take(received.reshape(groups * per_src, rb_local, BLK, BLK), order, axis=0)

    my_blocks = pan_idx * rb_local + jnp.arange(rb_local, dtype=jnp.int32)
    front_live = lax.dynamic_index_in_dim(front_blocks, group_idx, 0, keepdims=False)
    alive_rows = jnp.repeat(my_blocks < front_live, BLK)
    inverse_pivot = pivot_inverse[0]
    scaled = jnp.dot(panel[0], inverse_pivot, preferred_element_type=jnp.float32)
    scaled = jnp.where(alive_rows[:, None], scaled, jnp.zeros_like(scaled)).astype(jnp.bfloat16)
    full = lax.all_gather(scaled, "pan", axis=0, tiled=True)
    product = lax.dot_general(
        sigma,
        full.reshape(front_len, BLK, P_SIZE),
        (((0, 2), (0, 1)), ((), ())),
        preferred_element_type=jnp.float32,
    ).reshape(rb_local * BLK, P_SIZE)
    cross = jnp.where(alive_rows[:, None], -product, jnp.zeros_like(product)).astype(jnp.bfloat16)
    pivot_rows = P_SIZE // pan_count
    part = (-lax.dot_general(scaled, cross, contract, preferred_element_type=jnp.float32)).astype(
        jnp.bfloat16
    )
    shared = scatter_sum(part.reshape(pan_count, pivot_rows, P_SIZE), pan_count)
    own_columns = lax.dynamic_slice_in_dim(inverse_pivot, pan_idx * pivot_rows, pivot_rows, 1)
    triangle = lax.dot_general(
        own_columns, inverse_pivot, contract, preferred_element_type=jnp.float32
    )
    triangle, shared = lax.optimization_barrier((triangle, shared))
    pivot = triangle + shared
    return (cross[None], pivot[None])


def solution(mesh):
    placed = (P("grp", "pan"), P(), P(), P(), P("grp", "pan", None), P("grp", None, None))
    return jax.shard_map(
        per_device,
        mesh=mesh,
        in_specs=placed,
        out_specs=(P("grp", "pan", None), P("grp", "pan", None)),
        check_vma=False,
    )
```

```python
import functools

import jax
import jax.numpy as jnp
from jax import lax
from jax.sharding import PartitionSpec as P
from jax.experimental import pallas as pl
from jax.experimental.pallas import tpu as pltpu

BLK = 128
P_SIZE = 768


PAN_INNER = 4


def _scatter_sum_kernel(
    inner, outer, part_ref, out_ref, first, mid, second, sems, local_sem
):
    me = lax.axis_index("pan")
    grp = lax.axis_index("grp")
    row, col = me // inner, me % inner
    mesh_ids = pl.DeviceIdType.MESH
    send1, recv1, send2, recv2 = sems

    barrier = pltpu.get_barrier_semaphore()

    def greet_row(k, carry):
        peer = row * inner + lax.rem(col + k, inner)
        pl.semaphore_signal(barrier, 1, device_id=(grp, peer), device_id_type=mesh_ids)
        return carry

    def greet_col(k, carry):
        peer = lax.rem(row + k, outer) * inner + col
        pl.semaphore_signal(barrier, 1, device_id=(grp, peer), device_id_type=mesh_ids)
        return carry

    for k in range(1, inner):
        greet_row(k, 0)
    for k in range(1, outer):
        greet_col(k, 0)
    pl.semaphore_wait(barrier, inner + outer - 2)

    own = pltpu.make_async_copy(part_ref.at[:, col], first.at[0], local_sem)
    own.start()

    def stage_one(k):
        dest = lax.rem(col + k, inner)
        return pltpu.make_async_remote_copy(
            src_ref=part_ref.at[:, dest],
            dst_ref=first.at[k],
            send_sem=send1.at[k],
            recv_sem=recv1.at[k],
            device_id=(grp, row * inner + dest),
            device_id_type=mesh_ids,
        )

    def start_one(k, carry):
        stage_one(k).start()
        return carry

    def finish_one(k, carry):
        stage_one(k).wait()
        return carry

    for k in range(1, inner):
        start_one(k, 0)
    own.wait()
    for k in range(1, inner):
        finish_one(k, 0)

    mid[...] = first[0].astype(jnp.float32)

    def add_first(k, carry):
        mid[...] += first[k].astype(jnp.float32)
        return carry

    for k in range(1, inner):
        add_first(k, 0)

    def stage_two(k):
        dest = lax.rem(row + k, outer)
        return pltpu.make_async_remote_copy(
            src_ref=mid.at[dest],
            dst_ref=second.at[k],
            send_sem=send2.at[k],
            recv_sem=recv2.at[k],
            device_id=(grp, dest * inner + col),
            device_id_type=mesh_ids,
        )

    def start_two(k, carry):
        stage_two(k).start()
        return carry

    def finish_two(k, carry):
        stage_two(k).wait()
        return carry

    for k in range(1, outer):
        start_two(k, 0)
    for k in range(1, outer):
        finish_two(k, 0)

    out_ref[...] = mid[row]

    def add_second(k, carry):
        out_ref[...] += second[k]
        return carry

    for k in range(1, outer):
        add_second(k, 0)


def scatter_sum(part, n):
    _, rows, cols = part.shape
    inner = PAN_INNER
    outer = n // inner
    return pl.pallas_call(
        functools.partial(_scatter_sum_kernel, inner, outer),
        out_shape=jax.ShapeDtypeStruct((rows, cols), jnp.float32),
        in_specs=[pl.BlockSpec(memory_space=pl.ANY)],
        out_specs=pl.BlockSpec(memory_space=pltpu.VMEM),
        scratch_shapes=[
            pltpu.VMEM((inner, outer, rows, cols), part.dtype),
            pltpu.VMEM((outer, rows, cols), jnp.float32),
            pltpu.VMEM((outer, rows, cols), jnp.float32),
            (
                pltpu.SemaphoreType.DMA((inner,)),
                pltpu.SemaphoreType.DMA((inner,)),
                pltpu.SemaphoreType.DMA((outer,)),
                pltpu.SemaphoreType.DMA((outer,)),
            ),
            pltpu.SemaphoreType.DMA,
        ],
        compiler_params=pltpu.CompilerParams(collective_id=0, has_side_effects=True),
    )(part.reshape(outer, inner, rows, cols))


def per_device(anc_rows, row_home, block_lists, front_blocks, panel, pivot_inverse):
    groups = lax.axis_size("grp")
    pan_count = lax.axis_size("pan")
    group_idx = lax.axis_index("grp")
    pan_idx = lax.axis_index("pan")
    block_count = row_home.shape[0]
    front_len = block_lists.shape[1]
    rb_local = front_len // pan_count
    cb_local = anc_rows.shape[1] // BLK
    stored_blocks = anc_rows.shape[0] // BLK
    windows = block_count // cb_local
    win_per_group = windows // groups
    per_src = win_per_group * rb_local
    contract = (((0,), (0,)), ((), ()))

    home_of_window = row_home[cb_local * jnp.arange(windows, dtype=jnp.int32)] // stored_blocks
    win = jnp.argsort(home_of_window * windows + jnp.arange(windows, dtype=jnp.int32))
    win = win.reshape(groups, win_per_group).astype(jnp.int32)
    pos = (rb_local * win[:, :, None] + jnp.arange(rb_local, dtype=jnp.int32)).reshape(
        groups, per_src
    )

    my_pos = lax.dynamic_index_in_dim(pos, group_idx, 0, keepdims=False)
    row_blocks = jnp.take(block_lists, my_pos, axis=1)
    slots = jnp.take(row_home, row_blocks) - stored_blocks * group_idx
    cols = lax.dynamic_slice_in_dim(block_lists, rb_local * pan_idx, rb_local, axis=1) - (
        cb_local * pan_idx
    )
    local = anc_rows.reshape(stored_blocks, BLK, cb_local, BLK)
    outgoing = local[slots[:, :, None], :, cols[:, None, :], :]
    received = lax.all_to_all(outgoing, "grp", split_axis=0, concat_axis=0, tiled=True)
    order = jnp.argsort(pos.reshape(groups * per_src)).astype(jnp.int32)
    sigma = jnp.take(received.reshape(groups * per_src, rb_local, BLK, BLK), order, axis=0)

    my_blocks = pan_idx * rb_local + jnp.arange(rb_local, dtype=jnp.int32)
    front_live = lax.dynamic_index_in_dim(front_blocks, group_idx, 0, keepdims=False)
    alive_rows = jnp.repeat(my_blocks < front_live, BLK)
    inverse_pivot = pivot_inverse[0]
    scaled = jnp.dot(panel[0], inverse_pivot, preferred_element_type=jnp.float32)
    scaled = jnp.where(alive_rows[:, None], scaled, jnp.zeros_like(scaled)).astype(jnp.bfloat16)
    full = lax.all_gather(scaled, "pan", axis=0, tiled=True)
    product = lax.dot_general(
        sigma,
        full.reshape(front_len, BLK, P_SIZE),
        (((0, 2), (0, 1)), ((), ())),
        preferred_element_type=jnp.float32,
    ).reshape(rb_local * BLK, P_SIZE)
    cross = jnp.where(alive_rows[:, None], -product, jnp.zeros_like(product)).astype(jnp.bfloat16)
    pivot_rows = P_SIZE // pan_count
    part = (-lax.dot_general(scaled, cross, contract, preferred_element_type=jnp.float32)).astype(
        jnp.bfloat16
    )
    shared = scatter_sum(part.reshape(pan_count, pivot_rows, P_SIZE), pan_count)
    own_columns = lax.dynamic_slice_in_dim(inverse_pivot, pan_idx * pivot_rows, pivot_rows, 1)
    triangle = lax.dot_general(
        own_columns, inverse_pivot, contract, preferred_element_type=jnp.float32
    )
    triangle, shared = lax.optimization_barrier((triangle, shared))
    pivot = triangle + shared
    return (cross[None], pivot[None])


def solution(mesh):
    placed = (P("grp", "pan"), P(), P(), P(), P("grp", "pan", None), P("grp", None, None))
    return jax.shard_map(
        per_device,
        mesh=mesh,
        in_specs=placed,
        out_specs=(P("grp", "pan", None), P("grp", "pan", None)),
        check_vma=False,
    )
```

```python
import functools

import jax
import jax.numpy as jnp
from jax import lax
from jax.sharding import PartitionSpec as P
from jax.experimental import pallas as pl
from jax.experimental.pallas import tpu as pltpu

BLK = 128
P_SIZE = 768


PAN_INNER = 4


def _scatter_sum_kernel(
    inner, outer, scaled_ref, cross_ref, out_ref, part_ref, first, mid, second, sems, local_sem
):
    me = lax.axis_index("pan")
    grp = lax.axis_index("grp")
    row, col = me // inner, me % inner
    mesh_ids = pl.DeviceIdType.MESH
    send1, recv1, send2, recv2 = sems

    barrier = pltpu.get_barrier_semaphore()

    def greet_row(k, carry):
        peer = row * inner + lax.rem(col + k, inner)
        pl.semaphore_signal(barrier, 1, device_id=(grp, peer), device_id_type=mesh_ids)
        return carry

    def greet_col(k, carry):
        peer = lax.rem(row + k, outer) * inner + col
        pl.semaphore_signal(barrier, 1, device_id=(grp, peer), device_id_type=mesh_ids)
        return carry

    for k in range(1, inner):
        greet_row(k, 0)
    for k in range(1, outer):
        greet_col(k, 0)
    pl.semaphore_wait(barrier, inner + outer - 2)

    rows = part_ref.shape[2]
    part = -lax.dot_general(
        scaled_ref[...], cross_ref[...], (((0,), (0,)), ((), ())),
        preferred_element_type=jnp.float32,
    )
    for o in range(outer):
        for i in range(inner):
            slab = o * inner + i
            part_ref[o, i] = part[slab * rows : (slab + 1) * rows].astype(part_ref.dtype)

    own = pltpu.make_async_copy(part_ref.at[:, col], first.at[0], local_sem)
    own.start()

    def stage_one(k):
        dest = lax.rem(col + k, inner)
        return pltpu.make_async_remote_copy(
            src_ref=part_ref.at[:, dest],
            dst_ref=first.at[k],
            send_sem=send1.at[k],
            recv_sem=recv1.at[k],
            device_id=(grp, row * inner + dest),
            device_id_type=mesh_ids,
        )

    def start_one(k, carry):
        stage_one(k).start()
        return carry

    def finish_one(k, carry):
        stage_one(k).wait()
        return carry

    for k in range(1, inner):
        start_one(k, 0)
    own.wait()
    for k in range(1, inner):
        finish_one(k, 0)

    mid[...] = first[0].astype(jnp.float32)

    def add_first(k, carry):
        mid[...] += first[k].astype(jnp.float32)
        return carry

    for k in range(1, inner):
        add_first(k, 0)

    def stage_two(k):
        dest = lax.rem(row + k, outer)
        return pltpu.make_async_remote_copy(
            src_ref=mid.at[dest],
            dst_ref=second.at[k],
            send_sem=send2.at[k],
            recv_sem=recv2.at[k],
            device_id=(grp, dest * inner + col),
            device_id_type=mesh_ids,
        )

    def start_two(k, carry):
        stage_two(k).start()
        return carry

    def finish_two(k, carry):
        stage_two(k).wait()
        return carry

    for k in range(1, outer):
        start_two(k, 0)
    for k in range(1, outer):
        finish_two(k, 0)

    out_ref[...] = mid[row]

    def add_second(k, carry):
        out_ref[...] += second[k]
        return carry

    for k in range(1, outer):
        add_second(k, 0)


def scatter_sum(scaled, cross, n):
    cols = cross.shape[1]
    rows = scaled.shape[1] // n
    inner = PAN_INNER
    outer = n // inner
    return pl.pallas_call(
        functools.partial(_scatter_sum_kernel, inner, outer),
        out_shape=jax.ShapeDtypeStruct((rows, cols), jnp.float32),
        in_specs=[pl.BlockSpec(memory_space=pltpu.VMEM), pl.BlockSpec(memory_space=pltpu.VMEM)],
        out_specs=pl.BlockSpec(memory_space=pltpu.VMEM),
        scratch_shapes=[
            pltpu.VMEM((outer, inner, rows, cols), cross.dtype),
            pltpu.VMEM((inner, outer, rows, cols), cross.dtype),
            pltpu.VMEM((outer, rows, cols), jnp.float32),
            pltpu.VMEM((outer, rows, cols), jnp.float32),
            (
                pltpu.SemaphoreType.DMA((inner,)),
                pltpu.SemaphoreType.DMA((inner,)),
                pltpu.SemaphoreType.DMA((outer,)),
                pltpu.SemaphoreType.DMA((outer,)),
            ),
            pltpu.SemaphoreType.DMA,
        ],
        compiler_params=pltpu.CompilerParams(collective_id=0, has_side_effects=True),
    )(scaled, cross)


def per_device(anc_rows, row_home, block_lists, front_blocks, panel, pivot_inverse):
    groups = lax.axis_size("grp")
    pan_count = lax.axis_size("pan")
    group_idx = lax.axis_index("grp")
    pan_idx = lax.axis_index("pan")
    block_count = row_home.shape[0]
    front_len = block_lists.shape[1]
    rb_local = front_len // pan_count
    cb_local = anc_rows.shape[1] // BLK
    stored_blocks = anc_rows.shape[0] // BLK
    windows = block_count // cb_local
    win_per_group = windows // groups
    per_src = win_per_group * rb_local
    contract = (((0,), (0,)), ((), ()))

    home_of_window = row_home[cb_local * jnp.arange(windows, dtype=jnp.int32)] // stored_blocks
    win = jnp.argsort(home_of_window * windows + jnp.arange(windows, dtype=jnp.int32))
    win = win.reshape(groups, win_per_group).astype(jnp.int32)
    pos = (rb_local * win[:, :, None] + jnp.arange(rb_local, dtype=jnp.int32)).reshape(
        groups, per_src
    )

    my_pos = lax.dynamic_index_in_dim(pos, group_idx, 0, keepdims=False)
    row_blocks = jnp.take(block_lists, my_pos, axis=1)
    slots = jnp.take(row_home, row_blocks) - stored_blocks * group_idx
    cols = lax.dynamic_slice_in_dim(block_lists, rb_local * pan_idx, rb_local, axis=1) - (
        cb_local * pan_idx
    )
    local = anc_rows.reshape(stored_blocks, BLK, cb_local, BLK)
    outgoing = local[slots[:, :, None], :, cols[:, None, :], :]
    received = lax.all_to_all(outgoing, "grp", split_axis=0, concat_axis=0, tiled=True)
    order = jnp.argsort(pos.reshape(groups * per_src)).astype(jnp.int32)
    sigma = jnp.take(received.reshape(groups * per_src, rb_local, BLK, BLK), order, axis=0)

    my_blocks = pan_idx * rb_local + jnp.arange(rb_local, dtype=jnp.int32)
    front_live = lax.dynamic_index_in_dim(front_blocks, group_idx, 0, keepdims=False)
    alive_rows = jnp.repeat(my_blocks < front_live, BLK)
    inverse_pivot = pivot_inverse[0]
    scaled = jnp.dot(panel[0], inverse_pivot, preferred_element_type=jnp.float32)
    scaled = jnp.where(alive_rows[:, None], scaled, jnp.zeros_like(scaled)).astype(jnp.bfloat16)
    full = lax.all_gather(scaled, "pan", axis=0, tiled=True)
    product = lax.dot_general(
        sigma,
        full.reshape(front_len, BLK, P_SIZE),
        (((0, 2), (0, 1)), ((), ())),
        preferred_element_type=jnp.float32,
    ).reshape(rb_local * BLK, P_SIZE)
    cross = jnp.where(alive_rows[:, None], -product, jnp.zeros_like(product)).astype(jnp.bfloat16)
    pivot_rows = P_SIZE // pan_count
    shared = scatter_sum(scaled, cross, pan_count)
    own_columns = lax.dynamic_slice_in_dim(inverse_pivot, pan_idx * pivot_rows, pivot_rows, 1)
    triangle = lax.dot_general(
        own_columns, inverse_pivot, contract, preferred_element_type=jnp.float32
    )
    triangle, shared = lax.optimization_barrier((triangle, shared))
    pivot = triangle + shared
    return (cross[None], pivot[None])


def solution(mesh):
    placed = (P("grp", "pan"), P(), P(), P(), P("grp", "pan", None), P("grp", None, None))
    return jax.shard_map(
        per_device,
        mesh=mesh,
        in_specs=placed,
        out_specs=(P("grp", "pan", None), P("grp", "pan", None)),
        check_vma=False,
    )
```

```python
import functools

import jax
import jax.numpy as jnp
from jax import lax
from jax.sharding import PartitionSpec as P
from jax.experimental import pallas as pl
from jax.experimental.pallas import tpu as pltpu

BLK = 128
P_SIZE = 768


PAN_INNER = 4


def _scatter_sum_kernel(
    inner, outer, part_ref, out_ref, first, mid, second, sems, local_sem
):
    me = lax.axis_index("pan")
    grp = lax.axis_index("grp")
    row, col = me // inner, me % inner
    mesh_ids = pl.DeviceIdType.MESH
    send1, recv1, send2, recv2 = sems

    barrier = pltpu.get_barrier_semaphore()

    def greet_row(k, carry):
        peer = row * inner + lax.rem(col + k, inner)
        pl.semaphore_signal(barrier, 1, device_id=(grp, peer), device_id_type=mesh_ids)
        return carry

    def greet_col(k, carry):
        peer = lax.rem(row + k, outer) * inner + col
        pl.semaphore_signal(barrier, 1, device_id=(grp, peer), device_id_type=mesh_ids)
        return carry

    for k in range(1, inner):
        greet_row(k, 0)
    for k in range(1, outer):
        greet_col(k, 0)
    pl.semaphore_wait(barrier, inner + outer - 2)

    own = pltpu.make_async_copy(part_ref.at[:, col], first.at[0], local_sem)
    own.start()

    def stage_one(k):
        dest = lax.rem(col + k, inner)
        return pltpu.make_async_remote_copy(
            src_ref=part_ref.at[:, dest],
            dst_ref=first.at[k],
            send_sem=send1.at[k],
            recv_sem=recv1.at[k],
            device_id=(grp, row * inner + dest),
            device_id_type=mesh_ids,
        )

    def start_one(k, carry):
        stage_one(k).start()
        return carry

    def finish_one(k, carry):
        stage_one(k).wait()
        return carry

    for k in range(1, inner):
        start_one(k, 0)
    own.wait()
    for k in range(1, inner):
        finish_one(k, 0)

    mid[...] = first[0].astype(jnp.float32)

    def add_first(k, carry):
        mid[...] += first[k].astype(jnp.float32)
        return carry

    for k in range(1, inner):
        add_first(k, 0)

    def stage_two(k):
        dest = lax.rem(row + k, outer)
        return pltpu.make_async_remote_copy(
            src_ref=mid.at[dest],
            dst_ref=second.at[k],
            send_sem=send2.at[k],
            recv_sem=recv2.at[k],
            device_id=(grp, dest * inner + col),
            device_id_type=mesh_ids,
        )

    def start_two(k, carry):
        stage_two(k).start()
        return carry

    def finish_two(k, carry):
        stage_two(k).wait()
        return carry

    for k in range(1, outer):
        start_two(k, 0)
    for k in range(1, outer):
        finish_two(k, 0)

    out_ref[...] = mid[row]

    def add_second(k, carry):
        out_ref[...] += second[k]
        return carry

    for k in range(1, outer):
        add_second(k, 0)


def scatter_sum(part, n):
    _, rows, cols = part.shape
    inner = PAN_INNER
    outer = n // inner
    return pl.pallas_call(
        functools.partial(_scatter_sum_kernel, inner, outer),
        out_shape=jax.ShapeDtypeStruct((rows, cols), jnp.float32),
        in_specs=[pl.BlockSpec(memory_space=pl.ANY)],
        out_specs=pl.BlockSpec(memory_space=pltpu.VMEM),
        scratch_shapes=[
            pltpu.VMEM((inner, outer, rows, cols), part.dtype),
            pltpu.VMEM((outer, rows, cols), jnp.float32),
            pltpu.VMEM((outer, rows, cols), jnp.float32),
            (
                pltpu.SemaphoreType.DMA((inner,)),
                pltpu.SemaphoreType.DMA((inner,)),
                pltpu.SemaphoreType.DMA((outer,)),
                pltpu.SemaphoreType.DMA((outer,)),
            ),
            pltpu.SemaphoreType.DMA,
        ],
        compiler_params=pltpu.CompilerParams(collective_id=0, has_side_effects=True),
    )(part.reshape(outer, inner, rows, cols))


def per_device(anc_rows, row_home, block_lists, front_blocks, panel, pivot_inverse):
    groups = lax.axis_size("grp")
    pan_count = lax.axis_size("pan")
    group_idx = lax.axis_index("grp")
    pan_idx = lax.axis_index("pan")
    block_count = row_home.shape[0]
    front_len = block_lists.shape[1]
    rb_local = front_len // pan_count
    cb_local = anc_rows.shape[1] // BLK
    stored_blocks = anc_rows.shape[0] // BLK
    windows = block_count // cb_local
    win_per_group = windows // groups
    per_src = win_per_group * rb_local
    contract = (((0,), (0,)), ((), ()))

    home_of_window = row_home[cb_local * jnp.arange(windows, dtype=jnp.int32)] // stored_blocks
    win = jnp.argsort(home_of_window * windows + jnp.arange(windows, dtype=jnp.int32))
    win = win.reshape(groups, win_per_group).astype(jnp.int32)
    pos = (rb_local * win[:, :, None] + jnp.arange(rb_local, dtype=jnp.int32)).reshape(
        groups, per_src
    )

    my_pos = lax.dynamic_index_in_dim(pos, group_idx, 0, keepdims=False)
    row_blocks = jnp.take(block_lists, my_pos, axis=1)
    slots = jnp.take(row_home, row_blocks) - stored_blocks * group_idx
    cols = lax.dynamic_slice_in_dim(block_lists, rb_local * pan_idx, rb_local, axis=1) - (
        cb_local * pan_idx
    )
    local = anc_rows.reshape(stored_blocks, BLK, cb_local, BLK)
    outgoing = local[slots[:, :, None], :, cols[:, None, :], :]
    received = lax.all_to_all(outgoing, "grp", split_axis=0, concat_axis=0, tiled=True)
    order = jnp.argsort(pos.reshape(groups * per_src)).astype(jnp.int32)
    sigma = jnp.take(received.reshape(groups * per_src, rb_local, BLK, BLK), order, axis=0)

    my_blocks = pan_idx * rb_local + jnp.arange(rb_local, dtype=jnp.int32)
    front_live = lax.dynamic_index_in_dim(front_blocks, group_idx, 0, keepdims=False)
    alive_rows = jnp.repeat(my_blocks < front_live, BLK)
    inverse_pivot = pivot_inverse[0]
    raw = jnp.dot(panel[0], inverse_pivot, preferred_element_type=jnp.float32).astype(jnp.bfloat16)
    full = lax.all_gather(raw, "pan", axis=0, tiled=True)
    scaled = jnp.where(alive_rows[:, None], raw, jnp.zeros_like(raw))
    alive_blocks = jnp.arange(front_len, dtype=jnp.int32) < front_live
    sigma = jnp.where(alive_blocks[:, None, None, None], sigma, jnp.zeros_like(sigma))
    product = lax.dot_general(
        sigma,
        full.reshape(front_len, BLK, P_SIZE),
        (((0, 2), (0, 1)), ((), ())),
        preferred_element_type=jnp.float32,
    ).reshape(rb_local * BLK, P_SIZE)
    cross = jnp.where(alive_rows[:, None], -product, jnp.zeros_like(product)).astype(jnp.bfloat16)
    pivot_rows = P_SIZE // pan_count
    part = (-lax.dot_general(scaled, cross, contract, preferred_element_type=jnp.float32)).astype(
        jnp.bfloat16
    )
    shared = scatter_sum(part.reshape(pan_count, pivot_rows, P_SIZE), pan_count)
    own_columns = lax.dynamic_slice_in_dim(inverse_pivot, pan_idx * pivot_rows, pivot_rows, 1)
    triangle = lax.dot_general(
        own_columns, inverse_pivot, contract, preferred_element_type=jnp.float32
    )
    triangle, shared = lax.optimization_barrier((triangle, shared))
    pivot = triangle + shared
    return (cross[None], pivot[None])


def solution(mesh):
    placed = (P("grp", "pan"), P(), P(), P(), P("grp", "pan", None), P("grp", None, None))
    return jax.shard_map(
        per_device,
        mesh=mesh,
        in_specs=placed,
        out_specs=(P("grp", "pan", None), P("grp", "pan", None)),
        check_vma=False,
    )
```

```python
import functools

import jax
import jax.numpy as jnp
from jax import lax
from jax.sharding import PartitionSpec as P
from jax.experimental import pallas as pl
from jax.experimental.pallas import tpu as pltpu

BLK = 128
P_SIZE = 768


PAN_INNER = 4


def _scatter_sum_kernel(
    inner, outer, part_ref, out_ref, first, mid, mid_out, second, sems, local_sem
):
    me = lax.axis_index("pan")
    grp = lax.axis_index("grp")
    row, col = me // inner, me % inner
    mesh_ids = pl.DeviceIdType.MESH
    send1, recv1, send2, recv2 = sems

    barrier = pltpu.get_barrier_semaphore()

    def greet_row(k, carry):
        peer = row * inner + lax.rem(col + k, inner)
        pl.semaphore_signal(barrier, 1, device_id=(grp, peer), device_id_type=mesh_ids)
        return carry

    def greet_col(k, carry):
        peer = lax.rem(row + k, outer) * inner + col
        pl.semaphore_signal(barrier, 1, device_id=(grp, peer), device_id_type=mesh_ids)
        return carry

    for k in range(1, inner):
        greet_row(k, 0)
    for k in range(1, outer):
        greet_col(k, 0)
    pl.semaphore_wait(barrier, inner + outer - 2)

    own = pltpu.make_async_copy(part_ref.at[:, col], first.at[0], local_sem)
    own.start()

    def stage_one(k):
        dest = lax.rem(col + k, inner)
        return pltpu.make_async_remote_copy(
            src_ref=part_ref.at[:, dest],
            dst_ref=first.at[k],
            send_sem=send1.at[k],
            recv_sem=recv1.at[k],
            device_id=(grp, row * inner + dest),
            device_id_type=mesh_ids,
        )

    def start_one(k, carry):
        stage_one(k).start()
        return carry

    def finish_one(k, carry):
        stage_one(k).wait()
        return carry

    for k in range(1, inner):
        start_one(k, 0)
    own.wait()
    for k in range(1, inner):
        finish_one(k, 0)

    mid[...] = first[0].astype(jnp.float32)

    def add_first(k, carry):
        mid[...] += first[k].astype(jnp.float32)
        return carry

    for k in range(1, inner):
        add_first(k, 0)
    mid_out[...] = mid[...].astype(mid_out.dtype)

    def stage_two(k):
        dest = lax.rem(row + k, outer)
        return pltpu.make_async_remote_copy(
            src_ref=mid_out.at[dest],
            dst_ref=second.at[k],
            send_sem=send2.at[k],
            recv_sem=recv2.at[k],
            device_id=(grp, dest * inner + col),
            device_id_type=mesh_ids,
        )

    def start_two(k, carry):
        stage_two(k).start()
        return carry

    def finish_two(k, carry):
        stage_two(k).wait()
        return carry

    for k in range(1, outer):
        start_two(k, 0)
    for k in range(1, outer):
        finish_two(k, 0)

    out_ref[...] = mid[row]

    def add_second(k, carry):
        out_ref[...] += second[k].astype(jnp.float32)
        return carry

    for k in range(1, outer):
        add_second(k, 0)


def scatter_sum(part, n):
    _, rows, cols = part.shape
    inner = PAN_INNER
    outer = n // inner
    return pl.pallas_call(
        functools.partial(_scatter_sum_kernel, inner, outer),
        out_shape=jax.ShapeDtypeStruct((rows, cols), jnp.float32),
        in_specs=[pl.BlockSpec(memory_space=pl.ANY)],
        out_specs=pl.BlockSpec(memory_space=pltpu.VMEM),
        scratch_shapes=[
            pltpu.VMEM((inner, outer, rows, cols), part.dtype),
            pltpu.VMEM((outer, rows, cols), jnp.float32),
            pltpu.VMEM((outer, rows, cols), part.dtype),
            pltpu.VMEM((outer, rows, cols), part.dtype),
            (
                pltpu.SemaphoreType.DMA((inner,)),
                pltpu.SemaphoreType.DMA((inner,)),
                pltpu.SemaphoreType.DMA((outer,)),
                pltpu.SemaphoreType.DMA((outer,)),
            ),
            pltpu.SemaphoreType.DMA,
        ],
        compiler_params=pltpu.CompilerParams(collective_id=0, has_side_effects=True),
    )(part.reshape(outer, inner, rows, cols))


def per_device(anc_rows, row_home, block_lists, front_blocks, panel, pivot_inverse):
    groups = lax.axis_size("grp")
    pan_count = lax.axis_size("pan")
    group_idx = lax.axis_index("grp")
    pan_idx = lax.axis_index("pan")
    block_count = row_home.shape[0]
    front_len = block_lists.shape[1]
    rb_local = front_len // pan_count
    cb_local = anc_rows.shape[1] // BLK
    stored_blocks = anc_rows.shape[0] // BLK
    windows = block_count // cb_local
    win_per_group = windows // groups
    per_src = win_per_group * rb_local
    contract = (((0,), (0,)), ((), ()))

    home_of_window = row_home[cb_local * jnp.arange(windows, dtype=jnp.int32)] // stored_blocks
    win = jnp.argsort(home_of_window * windows + jnp.arange(windows, dtype=jnp.int32))
    win = win.reshape(groups, win_per_group).astype(jnp.int32)
    pos = (rb_local * win[:, :, None] + jnp.arange(rb_local, dtype=jnp.int32)).reshape(
        groups, per_src
    )

    my_pos = lax.dynamic_index_in_dim(pos, group_idx, 0, keepdims=False)
    row_blocks = jnp.take(block_lists, my_pos, axis=1)
    slots = jnp.take(row_home, row_blocks) - stored_blocks * group_idx
    cols = lax.dynamic_slice_in_dim(block_lists, rb_local * pan_idx, rb_local, axis=1) - (
        cb_local * pan_idx
    )
    local = anc_rows.reshape(stored_blocks, BLK, cb_local, BLK)
    outgoing = local[slots[:, :, None], :, cols[:, None, :], :]
    received = lax.all_to_all(outgoing, "grp", split_axis=0, concat_axis=0, tiled=True)
    order = jnp.argsort(pos.reshape(groups * per_src)).astype(jnp.int32)
    sigma = jnp.take(received.reshape(groups * per_src, rb_local, BLK, BLK), order, axis=0)

    my_blocks = pan_idx * rb_local + jnp.arange(rb_local, dtype=jnp.int32)
    front_live = lax.dynamic_index_in_dim(front_blocks, group_idx, 0, keepdims=False)
    alive_rows = jnp.repeat(my_blocks < front_live, BLK)
    inverse_pivot = pivot_inverse[0]
    scaled = jnp.dot(panel[0], inverse_pivot, preferred_element_type=jnp.float32)
    scaled = jnp.where(alive_rows[:, None], scaled, jnp.zeros_like(scaled)).astype(jnp.bfloat16)
    full = lax.all_gather(scaled, "pan", axis=0, tiled=True)
    product = lax.dot_general(
        sigma,
        full.reshape(front_len, BLK, P_SIZE),
        (((0, 2), (0, 1)), ((), ())),
        preferred_element_type=jnp.float32,
    ).reshape(rb_local * BLK, P_SIZE)
    cross = jnp.where(alive_rows[:, None], -product, jnp.zeros_like(product)).astype(jnp.bfloat16)
    pivot_rows = P_SIZE // pan_count
    part = (-lax.dot_general(scaled, cross, contract, preferred_element_type=jnp.float32)).astype(
        jnp.bfloat16
    )
    shared = scatter_sum(part.reshape(pan_count, pivot_rows, P_SIZE), pan_count)
    own_columns = lax.dynamic_slice_in_dim(inverse_pivot, pan_idx * pivot_rows, pivot_rows, 1)
    triangle = lax.dot_general(
        own_columns, inverse_pivot, contract, preferred_element_type=jnp.float32
    )
    triangle, shared = lax.optimization_barrier((triangle, shared))
    pivot = triangle + shared
    return (cross[None], pivot[None])


def solution(mesh):
    placed = (P("grp", "pan"), P(), P(), P(), P("grp", "pan", None), P("grp", None, None))
    return jax.shard_map(
        per_device,
        mesh=mesh,
        in_specs=placed,
        out_specs=(P("grp", "pan", None), P("grp", "pan", None)),
        check_vma=False,
    )
```

```python
import functools

import jax
import jax.numpy as jnp
from jax import lax
from jax.sharding import PartitionSpec as P
from jax.experimental import pallas as pl
from jax.experimental.pallas import tpu as pltpu

BLK = 128
P_SIZE = 768


PAN_INNER = 4


def _scatter_sum_kernel(
    inner, outer, part_ref, out_ref, first, mid, mid_out, second, sems, local_sem
):
    me = lax.axis_index("pan")
    grp = lax.axis_index("grp")
    row, col = me // inner, me % inner
    mesh_ids = pl.DeviceIdType.MESH
    send1, recv1, send2, recv2 = sems

    barrier = pltpu.get_barrier_semaphore()

    def greet_row(k, carry):
        peer = row * inner + lax.rem(col + k, inner)
        pl.semaphore_signal(barrier, 1, device_id=(grp, peer), device_id_type=mesh_ids)
        return carry

    def greet_col(k, carry):
        peer = lax.rem(row + k, outer) * inner + col
        pl.semaphore_signal(barrier, 1, device_id=(grp, peer), device_id_type=mesh_ids)
        return carry

    for k in range(1, inner):
        greet_row(k, 0)
    for k in range(1, outer):
        greet_col(k, 0)
    pl.semaphore_wait(barrier, inner + outer - 2)

    own = pltpu.make_async_copy(part_ref.at[:, col], first.at[0], local_sem)
    own.start()

    def stage_one(k):
        dest = lax.rem(col + k, inner)
        return pltpu.make_async_remote_copy(
            src_ref=part_ref.at[:, dest],
            dst_ref=first.at[k],
            send_sem=send1.at[k],
            recv_sem=recv1.at[k],
            device_id=(grp, row * inner + dest),
            device_id_type=mesh_ids,
        )

    def start_one(k, carry):
        stage_one(k).start()
        return carry

    def finish_one(k, carry):
        stage_one(k).wait()
        return carry

    for k in range(1, inner):
        start_one(k, 0)
    own.wait()
    for k in range(1, inner):
        finish_one(k, 0)

    mid[...] = first[0].astype(jnp.float32)

    def add_first(k, carry):
        mid[...] += first[k].astype(jnp.float32)
        return carry

    for k in range(1, inner):
        add_first(k, 0)
    mid_out[...] = mid[...].astype(mid_out.dtype)

    def stage_two(k):
        dest = lax.rem(row + k, outer)
        return pltpu.make_async_remote_copy(
            src_ref=mid_out.at[dest],
            dst_ref=second.at[k],
            send_sem=send2.at[k],
            recv_sem=recv2.at[k],
            device_id=(grp, dest * inner + col),
            device_id_type=mesh_ids,
        )

    def start_two(k, carry):
        stage_two(k).start()
        return carry

    def finish_two(k, carry):
        stage_two(k).wait()
        return carry

    for k in range(1, outer):
        start_two(k, 0)
    for k in range(1, outer):
        finish_two(k, 0)

    out_ref[...] = mid[row]

    def add_second(k, carry):
        out_ref[...] += second[k].astype(jnp.float32)
        return carry

    for k in range(1, outer):
        add_second(k, 0)


def scatter_sum(part, n):
    _, rows, cols = part.shape
    inner = PAN_INNER
    outer = n // inner
    return pl.pallas_call(
        functools.partial(_scatter_sum_kernel, inner, outer),
        out_shape=jax.ShapeDtypeStruct((rows, cols), jnp.float32),
        in_specs=[pl.BlockSpec(memory_space=pl.ANY)],
        out_specs=pl.BlockSpec(memory_space=pltpu.VMEM),
        scratch_shapes=[
            pltpu.VMEM((inner, outer, rows, cols), part.dtype),
            pltpu.VMEM((outer, rows, cols), jnp.float32),
            pltpu.VMEM((outer, rows, cols), part.dtype),
            pltpu.VMEM((outer, rows, cols), part.dtype),
            (
                pltpu.SemaphoreType.DMA((inner,)),
                pltpu.SemaphoreType.DMA((inner,)),
                pltpu.SemaphoreType.DMA((outer,)),
                pltpu.SemaphoreType.DMA((outer,)),
            ),
            pltpu.SemaphoreType.DMA,
        ],
        compiler_params=pltpu.CompilerParams(collective_id=0, has_side_effects=True),
    )(part.reshape(outer, inner, rows, cols))


def per_device(anc_rows, row_home, block_lists, front_blocks, panel, pivot_inverse):
    groups = lax.axis_size("grp")
    pan_count = lax.axis_size("pan")
    group_idx = lax.axis_index("grp")
    pan_idx = lax.axis_index("pan")
    block_count = row_home.shape[0]
    front_len = block_lists.shape[1]
    rb_local = front_len // pan_count
    cb_local = anc_rows.shape[1] // BLK
    stored_blocks = anc_rows.shape[0] // BLK
    windows = block_count // cb_local
    win_per_group = windows // groups
    per_src = win_per_group * rb_local
    contract = (((0,), (0,)), ((), ()))

    home_of_window = row_home[cb_local * jnp.arange(windows, dtype=jnp.int32)] // stored_blocks
    win = jnp.argsort(home_of_window * windows + jnp.arange(windows, dtype=jnp.int32))
    win = win.reshape(groups, win_per_group).astype(jnp.int32)
    pos = (rb_local * win[:, :, None] + jnp.arange(rb_local, dtype=jnp.int32)).reshape(
        groups, per_src
    )

    my_pos = lax.dynamic_index_in_dim(pos, group_idx, 0, keepdims=False)
    row_blocks = jnp.take(block_lists, my_pos, axis=1)
    slots = jnp.take(row_home, row_blocks) - stored_blocks * group_idx
    cols = lax.dynamic_slice_in_dim(block_lists, rb_local * pan_idx, rb_local, axis=1) - (
        cb_local * pan_idx
    )
    local = anc_rows.reshape(stored_blocks, BLK, cb_local, BLK)
    outgoing = local[slots[:, :, None], :, cols[:, None, :], :]
    received = lax.all_to_all(outgoing, "grp", split_axis=0, concat_axis=0, tiled=True)
    order = jnp.argsort(pos.reshape(groups * per_src)).astype(jnp.int32)
    sigma = jnp.take(received.reshape(groups * per_src, rb_local, BLK, BLK), order, axis=0)

    my_blocks = pan_idx * rb_local + jnp.arange(rb_local, dtype=jnp.int32)
    front_live = lax.dynamic_index_in_dim(front_blocks, group_idx, 0, keepdims=False)
    alive_rows = jnp.repeat(my_blocks < front_live, BLK)
    inverse_pivot = pivot_inverse[0]
    scaled = jnp.dot(panel[0], inverse_pivot, preferred_element_type=jnp.float32)
    scaled = jnp.where(alive_rows[:, None], scaled, jnp.zeros_like(scaled)).astype(jnp.bfloat16)
    full = lax.all_gather(scaled, "pan", axis=0, tiled=True)
    product = lax.dot_general(
        sigma,
        full.reshape(front_len, BLK, P_SIZE),
        (((0, 2), (0, 1)), ((), ())),
        preferred_element_type=jnp.float32,
    ).reshape(rb_local * BLK, P_SIZE)
    cross = jnp.where(alive_rows[:, None], -product, jnp.zeros_like(product)).astype(jnp.bfloat16)
    pivot_rows = P_SIZE // pan_count
    part = (-lax.dot_general(scaled, cross, contract, preferred_element_type=jnp.float32)).astype(
        jnp.bfloat16
    )
    slab_rows = pivot_rows * P_SIZE // BLK
    shared = scatter_sum(part.reshape(pan_count, slab_rows, BLK), pan_count).reshape(
        pivot_rows, P_SIZE
    )
    own_columns = lax.dynamic_slice_in_dim(inverse_pivot, pan_idx * pivot_rows, pivot_rows, 1)
    triangle = lax.dot_general(
        own_columns, inverse_pivot, contract, preferred_element_type=jnp.float32
    )
    triangle, shared = lax.optimization_barrier((triangle, shared))
    pivot = triangle + shared
    return (cross[None], pivot[None])


def solution(mesh):
    placed = (P("grp", "pan"), P(), P(), P(), P("grp", "pan", None), P("grp", None, None))
    return jax.shard_map(
        per_device,
        mesh=mesh,
        in_specs=placed,
        out_specs=(P("grp", "pan", None), P("grp", "pan", None)),
        check_vma=False,
    )
```

```python
import functools

import jax
import jax.numpy as jnp
from jax import lax
from jax.sharding import PartitionSpec as P
from jax.experimental import pallas as pl
from jax.experimental.pallas import tpu as pltpu

BLK = 128
P_SIZE = 768


PAN_INNER = 4


def _scatter_sum_kernel(
    inner, outer, part_ref, out_ref, first, mid, mid_out, second, sems, local_sem
):
    me = lax.axis_index("pan")
    grp = lax.axis_index("grp")
    row, col = me // inner, me % inner
    mesh_ids = pl.DeviceIdType.MESH
    send1, recv1, send2, recv2 = sems

    barrier = pltpu.get_barrier_semaphore()

    def greet_row(k, carry):
        peer = row * inner + lax.rem(col + k, inner)
        pl.semaphore_signal(barrier, 1, device_id=(grp, peer), device_id_type=mesh_ids)
        return carry

    def greet_col(k, carry):
        peer = lax.rem(row + k, outer) * inner + col
        pl.semaphore_signal(barrier, 1, device_id=(grp, peer), device_id_type=mesh_ids)
        return carry

    for k in range(1, inner):
        greet_row(k, 0)
    for k in range(1, outer):
        greet_col(k, 0)
    pl.semaphore_wait(barrier, inner + outer - 2)

    own = pltpu.make_async_copy(part_ref.at[col], first.at[0], local_sem)
    own.start()

    def stage_one(k):
        dest = lax.rem(col + k, inner)
        return pltpu.make_async_remote_copy(
            src_ref=part_ref.at[dest],
            dst_ref=first.at[k],
            send_sem=send1.at[k],
            recv_sem=recv1.at[k],
            device_id=(grp, row * inner + dest),
            device_id_type=mesh_ids,
        )

    def start_one(k, carry):
        stage_one(k).start()
        return carry

    def finish_one(k, carry):
        stage_one(k).wait()
        return carry

    for k in range(1, inner):
        start_one(k, 0)
    own.wait()
    for k in range(1, inner):
        finish_one(k, 0)

    mid[...] = first[0].astype(jnp.float32)

    def add_first(k, carry):
        mid[...] += first[k].astype(jnp.float32)
        return carry

    for k in range(1, inner):
        add_first(k, 0)
    rows = mid_out.shape[1]
    for o in range(outer):
        mid_out[o] = mid[o * rows : (o + 1) * rows].astype(mid_out.dtype)

    def stage_two(k):
        dest = lax.rem(row + k, outer)
        return pltpu.make_async_remote_copy(
            src_ref=mid_out.at[dest],
            dst_ref=second.at[k],
            send_sem=send2.at[k],
            recv_sem=recv2.at[k],
            device_id=(grp, dest * inner + col),
            device_id_type=mesh_ids,
        )

    def start_two(k, carry):
        stage_two(k).start()
        return carry

    def finish_two(k, carry):
        stage_two(k).wait()
        return carry

    for k in range(1, outer):
        start_two(k, 0)
    for k in range(1, outer):
        finish_two(k, 0)

    out_ref[...] = mid[pl.ds(pl.multiple_of(row * rows, 8), rows)]

    def add_second(k, carry):
        out_ref[...] += second[k].astype(jnp.float32)
        return carry

    for k in range(1, outer):
        add_second(k, 0)


def scatter_sum(part, n):
    _, rows, cols = part.shape
    inner = PAN_INNER
    outer = n // inner
    return pl.pallas_call(
        functools.partial(_scatter_sum_kernel, inner, outer),
        out_shape=jax.ShapeDtypeStruct((rows, cols), jnp.float32),
        in_specs=[pl.BlockSpec(memory_space=pl.ANY)],
        out_specs=pl.BlockSpec(memory_space=pltpu.VMEM),
        scratch_shapes=[
            pltpu.VMEM((inner, outer * rows, cols), part.dtype),
            pltpu.VMEM((outer * rows, cols), jnp.float32),
            pltpu.VMEM((outer, rows, cols), part.dtype),
            pltpu.VMEM((outer, rows, cols), part.dtype),
            (
                pltpu.SemaphoreType.DMA((inner,)),
                pltpu.SemaphoreType.DMA((inner,)),
                pltpu.SemaphoreType.DMA((outer,)),
                pltpu.SemaphoreType.DMA((outer,)),
            ),
            pltpu.SemaphoreType.DMA,
        ],
        compiler_params=pltpu.CompilerParams(collective_id=0, has_side_effects=True),
    )(part.reshape(inner, outer * rows, cols))


def per_device(anc_rows, row_home, block_lists, front_blocks, panel, pivot_inverse):
    groups = lax.axis_size("grp")
    pan_count = lax.axis_size("pan")
    group_idx = lax.axis_index("grp")
    pan_idx = lax.axis_index("pan")
    block_count = row_home.shape[0]
    front_len = block_lists.shape[1]
    rb_local = front_len // pan_count
    cb_local = anc_rows.shape[1] // BLK
    stored_blocks = anc_rows.shape[0] // BLK
    windows = block_count // cb_local
    win_per_group = windows // groups
    per_src = win_per_group * rb_local
    contract = (((0,), (0,)), ((), ()))

    home_of_window = row_home[cb_local * jnp.arange(windows, dtype=jnp.int32)] // stored_blocks
    win = jnp.argsort(home_of_window * windows + jnp.arange(windows, dtype=jnp.int32))
    win = win.reshape(groups, win_per_group).astype(jnp.int32)
    pos = (rb_local * win[:, :, None] + jnp.arange(rb_local, dtype=jnp.int32)).reshape(
        groups, per_src
    )

    my_pos = lax.dynamic_index_in_dim(pos, group_idx, 0, keepdims=False)
    row_blocks = jnp.take(block_lists, my_pos, axis=1)
    slots = jnp.take(row_home, row_blocks) - stored_blocks * group_idx
    cols = lax.dynamic_slice_in_dim(block_lists, rb_local * pan_idx, rb_local, axis=1) - (
        cb_local * pan_idx
    )
    local = anc_rows.reshape(stored_blocks, BLK, cb_local, BLK)
    outgoing = local[slots[:, :, None], :, cols[:, None, :], :]
    received = lax.all_to_all(outgoing, "grp", split_axis=0, concat_axis=0, tiled=True)
    order = jnp.argsort(pos.reshape(groups * per_src)).astype(jnp.int32)
    sigma = jnp.take(received.reshape(groups * per_src, rb_local, BLK, BLK), order, axis=0)

    my_blocks = pan_idx * rb_local + jnp.arange(rb_local, dtype=jnp.int32)
    front_live = lax.dynamic_index_in_dim(front_blocks, group_idx, 0, keepdims=False)
    alive_rows = jnp.repeat(my_blocks < front_live, BLK)
    inverse_pivot = pivot_inverse[0]
    scaled = jnp.dot(panel[0], inverse_pivot, preferred_element_type=jnp.float32)
    scaled = jnp.where(alive_rows[:, None], scaled, jnp.zeros_like(scaled)).astype(jnp.bfloat16)
    full = lax.all_gather(scaled, "pan", axis=0, tiled=True)
    product = lax.dot_general(
        sigma,
        full.reshape(front_len, BLK, P_SIZE),
        (((0, 2), (0, 1)), ((), ())),
        preferred_element_type=jnp.float32,
    ).reshape(rb_local * BLK, P_SIZE)
    cross = jnp.where(alive_rows[:, None], -product, jnp.zeros_like(product)).astype(jnp.bfloat16)
    pivot_rows = P_SIZE // pan_count
    outer = pan_count // PAN_INNER
    grid_order = jnp.transpose(
        scaled.reshape(-1, outer, PAN_INNER, pivot_rows), (0, 2, 1, 3)
    ).reshape(scaled.shape)
    part = (
        -lax.dot_general(grid_order, cross, contract, preferred_element_type=jnp.float32)
    ).astype(jnp.bfloat16)
    shared = scatter_sum(part.reshape(pan_count, pivot_rows, P_SIZE), pan_count)
    own_columns = lax.dynamic_slice_in_dim(inverse_pivot, pan_idx * pivot_rows, pivot_rows, 1)
    triangle = lax.dot_general(
        own_columns, inverse_pivot, contract, preferred_element_type=jnp.float32
    )
    triangle, shared = lax.optimization_barrier((triangle, shared))
    pivot = triangle + shared
    return (cross[None], pivot[None])


def solution(mesh):
    placed = (P("grp", "pan"), P(), P(), P(), P("grp", "pan", None), P("grp", None, None))
    return jax.shard_map(
        per_device,
        mesh=mesh,
        in_specs=placed,
        out_specs=(P("grp", "pan", None), P("grp", "pan", None)),
        check_vma=False,
    )
```
